32 devices in a mesh: group: 4 (over y, x), tile: 8 (over z, core).
Axes of the slice: x: 2, y: 2, z: 4, core: 2. Of those that a mesh axis runs over, the one named last changes fastest.
Arguments:
- velocity_u: float32 [4, 1024, 1024], P('group', 'tile'), may hold values from -6 to 6
- velocity_v: float32 [4, 1024, 1024], P('group', 'tile'), may hold values from -6 to 6
- tracer: float32 [4, 1024, 1024], P('group', 'tile'), may hold values from -6 to 6
- land: int32 [1024, 1024], P('tile'), may hold values 0 or 1
- tile_depth: int32 [64], replicated, may hold values from 1 to 4, 96 in all
- conv_one: bfloat16 [64, 3, 3, 3], replicated, may hold values from -1.25 to 1.25
- bias_one: float32 [64], replicated, may hold values from -3 to 3
- conv_two: bfloat16 [64, 64, 3, 3], replicated, may hold values from -0.25 to 0.25
- bias_two: float32 [64], replicated, may hold values from -3 to 3
- conv_three: bfloat16 [3, 64, 3, 3], replicated, may hold values from -0.25 to 0.25
- bias_three: float32 [3], replicated, may hold values from -3 to 3
Outputs:
- east_two: float32 [4, 1024, 1024], P('group', 'tile')
- north_two: float32 [4, 1024, 1024], P('group', 'tile')
- tracer_one: float32 [4, 1024, 1024], P('group', 'tile')
The draws below stay inside these ranges and needn't reach their ends.
Inputs may be any that keep to these rules, and one draw needn't show every extreme that they name: `land`: 1 marks water. `tile_depth`: the entries sum to exactly 96; some column is 4 levels deep.
All inputs are finite; a program needn't handle non-finite values. No bound on the sum of `land` on one device may be relied on, other than what follows from the above.
Results may differ from the reference program's by a relative error of at most 0.00083.
Values may be sent and summed in bfloat16 or wider, within the bound.
No kernel may reach another device: no remote copies, remote signals or barrier semaphores. Data moves between devices by JAX's collectives and lax.ppermute only.
A program may use at most 128 MiB of HBM per device.

```python
import math
import jax
import jax.numpy as jnp
import numpy as np
from jax import lax

TS = 128
NTY = 8
CH = 64
C_IN = 3
C_OUT = 3
WET_DEV = 3
LEV = 4
NX = 1024
NY = 1024
NTILES = 64
WET_TILES = 96
N_GROUP = 4
N_TILE = 8


def place_ends(drawn, key, low, largest):
    shape = drawn.shape
    spot = [jax.random.randint(jax.random.fold_in(key, axis), (), 0, shape[axis]) for axis in range(len(shape))]
    drawn = drawn.at[tuple(spot)].set(low)
    longest = shape.index(max(shape))
    spot[longest] = (spot[longest] + 1) % shape[longest]
    return drawn.at[tuple(spot)].set(largest)


def block_levels(stream_key, dims, pieces, least, largest):
    def one(dim, shards_of):
        heights = jax.random.uniform(jax.random.fold_in(jax.random.fold_in(stream_key, 6), dim), (shards_of,), jnp.float32, least / len(pieces), largest / len(pieces))
        return jnp.repeat(jnp.exp(heights), dims[dim] // shards_of).reshape((-1,) + (1,) * (len(dims) - dim - 1))

    gain = one(*pieces[0])
    for cut in pieces[1:]:
        gain = gain * one(*cut)
    return gain


def length_profile(amount, total, most, skew):
    loads = [(1 << 20) // math.isqrt(standing ** skew) + 1 for standing in range(2, amount + 1)]
    spare, holding = total - most - (amount - 1), [1] * (amount - 1)
    while spare > 0:
        free = [i for i in range(amount - 1) if holding[i] < most]
        mass, budget = sum([loads[i] for i in free]), spare
        for i in free:
            more = min(most - holding[i], max(1, budget * loads[i] // mass), spare)
            holding[i] = holding[i] + more
            spare = spare - more
    return np.array([most] + holding)


def uneven_parts(stream_key, number_of, total, bound, slope):
    if number_of == 2:
        one = jax.random.randint(stream_key, (), max(1, total - bound), min(bound, total - 1) + 1)
        return jnp.stack([one, total - one])
    tallies = jnp.asarray(length_profile(number_of, total, bound, slope), jnp.int32)
    couples = (number_of - 1) // 2
    donor, receiver = tallies[1:1 + 2 * couples:2], tallies[2:2 + 2 * couples:2]
    room = jnp.minimum(donor - 1, bound - receiver)
    shifted = jax.random.randint(jax.random.fold_in(stream_key, 1), (couples,), 0, 1 << 20) % (room + 1)
    tallies = tallies.at[1:1 + 2 * couples:2].set(donor - shifted).at[2:2 + 2 * couples:2].set(receiver + shifted)
    return tallies[jax.random.permutation(jax.random.fold_in(stream_key, 2), number_of)]


def bell_draw(own_key, dims, width, most, split=(), held_as=jnp.bfloat16):
    factor_of = block_levels(own_key, dims, split, -0.22, 0.18) if split else 1.0
    values = jax.random.normal(own_key, dims, jnp.float32) * width * factor_of
    return jnp.minimum(jnp.maximum(values, -most), most).astype(held_as)


def setup_inputs(seed: int = 0) -> dict:
    streams_of = jax.random.split(jax.random.key(seed), 12)
    velocity_u = bell_draw(streams_of[0], (LEV, NX, NY), 1.0, 6.0, ((0, 4), (1, 8)), jnp.float32)
    velocity_v = bell_draw(streams_of[1], (LEV, NX, NY), 1.0, 6.0, ((0, 4), (1, 8)), jnp.float32)
    tracer = bell_draw(streams_of[2], (LEV, NX, NY), 1.0, 6.0, ((0, 4), (1, 8)), jnp.float32)
    land = place_ends((jax.random.randint(streams_of[3], (NX, NY), 0, 8) < 7).astype(jnp.int32), jax.random.fold_in(streams_of[3], 1), 0, 1)
    tile_depth = uneven_parts(streams_of[4], NTILES, WET_TILES, LEV, 2).astype(jnp.int32)
    conv_one = bell_draw(streams_of[5], (CH, C_IN, 3, 3), (C_IN * 9) ** -0.5, 1.25)
    bias_one = bell_draw(streams_of[6], (CH,), 0.5, 3.0, (), jnp.float32)
    conv_two = bell_draw(streams_of[7], (CH, CH, 3, 3), (CH * 9) ** -0.5, 0.25)
    bias_two = bell_draw(streams_of[8], (CH,), 0.5, 3.0, (), jnp.float32)
    conv_three = bell_draw(streams_of[9], (C_OUT, CH, 3, 3), (CH * 9) ** -0.5, 0.25)
    bias_three = bell_draw(streams_of[10], (C_OUT,), 0.5, 3.0, (), jnp.float32)
    return dict(velocity_u=velocity_u, velocity_v=velocity_v, tracer=tracer, land=land, tile_depth=tile_depth, conv_one=conv_one, bias_one=bias_one, conv_two=conv_two, bias_two=bias_two, conv_three=conv_three, bias_three=bias_three)


time_step = 0.1
viscosity = 0.5
diffusivity = 0.5
eddy_gain = 0.5
coriolis_base = 0.2
coriolis_slope = 0.6


def east_diff(field):
    return 0.5 * (field[..., 2:, 1:-1] - field[..., :-2, 1:-1])


def north_diff(field):
    return 0.5 * (field[..., 1:-1, 2:] - field[..., 1:-1, :-2])


def laplace(field):
    return (field[..., 2:, 1:-1] + field[..., :-2, 1:-1] + field[..., 1:-1, 2:]
            + field[..., 1:-1, :-2] - 4.0 * field[..., 1:-1, 1:-1])


def advance(padded_east, padded_north, padded_tracer, active, coriolis):
    inner_east = padded_east[..., 1:-1, 1:-1]
    inner_north = padded_north[..., 1:-1, 1:-1]
    inner_tracer = padded_tracer[..., 1:-1, 1:-1]
    grad_east = east_diff(padded_tracer)
    grad_north = north_diff(padded_tracer)
    new_east = inner_east + time_step * active * (coriolis * inner_north - grad_east + viscosity * laplace(padded_east))
    new_north = inner_north + time_step * active * (-coriolis * inner_east - grad_north + viscosity * laplace(padded_north))
    new_tracer = inner_tracer + time_step * active * (-(inner_east * grad_east + inner_north * grad_north) + diffusivity * laplace(padded_tracer))
    return new_east, new_north, new_tracer


def convolve(source, kernel):
    return lax.conv_general_dilated(source.astype(jnp.float32), kernel.astype(jnp.float32), (1, 1), "VALID",
                                    dimension_numbers=("NCHW", "OIHW", "NCHW"), precision=lax.Precision.HIGHEST)


def closure(window, conv_one, bias_one, conv_two, bias_two, conv_three, bias_three):
    hidden_one = jax.nn.silu(convolve(window, conv_one) + bias_one[None, :, None, None]).astype(jnp.bfloat16)
    hidden_two = jax.nn.silu(convolve(hidden_one, conv_two) + bias_two[None, :, None, None]).astype(jnp.bfloat16)
    return (convolve(hidden_two, conv_three) + bias_three[None, :, None, None]).astype(jnp.bfloat16)


def reference(velocity_u, velocity_v, tracer, land, tile_depth, conv_one, bias_one, conv_two, bias_two, conv_three, bias_three):
    depth_grid = tile_depth.reshape(N_TILE, NTY)
    depth_cells = jnp.repeat(jnp.repeat(depth_grid, TS, axis=0), TS, axis=1)
    levels = jnp.arange(LEV, dtype=jnp.int32)
    active = ((land[None] == 1) & (levels[:, None, None] < depth_cells[None])).astype(jnp.float32)
    coriolis = (coriolis_base + coriolis_slope * (jnp.arange(NX, dtype=jnp.float32) + 0.5) / NX)[:, None]
    padded = jnp.pad(jnp.stack([velocity_u, velocity_v, tracer]), ((0, 0), (0, 0), (1, 1), (1, 1)))
    east_one, north_one, tracer_one = advance(padded[0], padded[1], padded[2], active, coriolis)
    features = (jnp.stack([east_one, north_one, tracer_one], axis=1) * active[:, None]).astype(jnp.bfloat16)
    framed = jnp.pad(features, ((0, 0), (0, 0), (3, 3), (3, 3)))
    wet_flags = (levels[:, None, None] < depth_grid[None]).astype(jnp.int32)
    order = jnp.argsort(1 - wet_flags.reshape(-1), stable=True)[: WET_DEV * N_GROUP * N_TILE].astype(jnp.int32)
    tiles_all = LEV * N_TILE * NTY

    def one_tile(index):
        level = index // (N_TILE * NTY)
        place = index % (N_TILE * NTY)
        row_tile = place // NTY
        col_tile = place % NTY
        window = lax.dynamic_slice(framed, (level, jnp.int32(0), row_tile * TS, col_tile * TS), (1, C_IN, TS + 6, TS + 6))
        return closure(window, conv_one, bias_one, conv_two, bias_two, conv_three, bias_three)[0]

    stresses = lax.map(one_tile, order)
    placed = jnp.zeros((tiles_all, C_OUT, TS, TS), jnp.bfloat16).at[order].set(stresses)
    stress = placed.reshape(LEV, N_TILE, NTY, C_OUT, TS, TS).transpose(0, 3, 1, 4, 2, 5).reshape(LEV, C_OUT, NX, NY)
    masked = (stress.astype(jnp.float32) * active[:, None]).astype(jnp.bfloat16)
    framed_stress = jnp.pad(masked.astype(jnp.float32), ((0, 0), (0, 0), (1, 1), (1, 1)))
    push_east = east_diff(framed_stress[:, 0]) + north_diff(framed_stress[:, 1])
    push_north = east_diff(framed_stress[:, 1]) + north_diff(framed_stress[:, 2])
    east_two = east_one + eddy_gain * active * push_east
    north_two = north_one + eddy_gain * active * push_north
    return east_two, north_two, tracer_one
```

```python
import functools

import jax
import jax.numpy as jnp
import numpy as np
from jax import lax
from jax.experimental import pallas as pl
from jax.experimental.pallas import tpu as pltpu
from jax.sharding import PartitionSpec as P

time_step = 0.1
viscosity = 0.5
diffusivity = 0.5
eddy_gain = 0.5
coriolis_base = 0.2
coriolis_slope = 0.6

LANES = 128
PITCH = 80
HALO = 4
WIN = 8


def east_diff(field):
    return 0.5 * (field[..., 2:, 1:-1] - field[..., :-2, 1:-1])


def north_diff(field):
    return 0.5 * (field[..., 1:-1, 2:] - field[..., 1:-1, :-2])


def laplace(field):
    return (
        field[..., 2:, 1:-1]
        + field[..., :-2, 1:-1]
        + field[..., 1:-1, 2:]
        + field[..., 1:-1, :-2]
        - 4.0 * field[..., 1:-1, 1:-1]
    )


def advance(padded_east, padded_north, padded_tracer, active, coriolis):
    inner_east = padded_east[..., 1:-1, 1:-1]
    inner_north = padded_north[..., 1:-1, 1:-1]
    inner_tracer = padded_tracer[..., 1:-1, 1:-1]
    grad_east = east_diff(padded_tracer)
    grad_north = north_diff(padded_tracer)
    new_east = inner_east + time_step * active * (
        coriolis * inner_north - grad_east + viscosity * laplace(padded_east)
    )
    new_north = inner_north + time_step * active * (
        -coriolis * inner_east - grad_north + viscosity * laplace(padded_north)
    )
    new_tracer = inner_tracer + time_step * active * (
        -(inner_east * grad_east + inner_north * grad_north) + diffusivity * laplace(padded_tracer)
    )
    return (new_east, new_north, new_tracer)


def extend_rows(block, width):
    count = lax.axis_size("tile")
    forward = [(i, i + 1) for i in range(count - 1)]
    backward = [(target, source) for source, target in forward]
    low = lax.ppermute(block[:, -width:], "tile", forward)
    high = lax.ppermute(block[:, :width], "tile", backward)
    return jnp.concatenate([low, block, high], axis=1)


def operators(rows_out):
    j = np.arange(LANES)
    w = np.arange(3 * LANES)
    rows_in = rows_out + 2 * HALO
    block_rows = rows_out // 2 + 1
    split = np.concatenate([w[:, None] == (2 * j - 5 + s + LANES)[None] for s in range(4)], axis=1)
    place = np.concatenate([2 * (j - 1) + par for par in range(2)])
    mask_columns = w[:, None] == (place + LANES)[None]
    merge = (place[:, None] == j[None]).astype(np.float32)
    slope = 0.5 * eddy_gain
    north = slope * (
        (place[:, None] == j[None] + 1).astype(np.float32)
        - (place[:, None] == j[None] - 1).astype(np.float32)
    )
    padded = -(-block_rows * 8 // 16) * 16
    index = np.arange(padded)
    row = 2 * (index // 8) - 1 + (index % 8) // 4
    comp = np.where(index < block_rows * 8, index % 4, 3)
    spread = row[:, None] == (np.arange(rows_in) - HALO)[None]
    out = np.arange(rows_out)
    first, second = [], []
    for output in range(2):
        ours = (comp == output)[None]
        first.append(
            slope
            * (
                (ours & (row[None] == out[:, None] + 1)).astype(np.float32)
                - (ours & (row[None] == out[:, None] - 1)).astype(np.float32)
            )
        )
        second.append(((comp == output + 1)[None] & (row[None] == out[:, None])).astype(np.float32))
    return [
        jnp.asarray(np.asarray(table, np.float32), jnp.bfloat16)
        for table in (split, mask_columns, merge, north, spread, np.concatenate(first), np.concatenate(second))
    ]


def taps(kernel):
    return jnp.stack(
        [
            jnp.stack(
                [
                    jnp.pad(kernel.transpose(2, 3, 0, 1), ((p, 1 - p), (par, 1 - par), (0, 0), (0, 0)))
                    for par in range(2)
                ],
                axis=2,
            )
            for p in range(2)
        ],
        axis=2,
    )


def arranged_weights(conv_one, bias_one, conv_two, bias_two, conv_three, bias_three):
    hidden, inputs = conv_one.shape[:2]
    outputs = conv_three.shape[0]
    half = jnp.asarray(0.5, jnp.bfloat16)
    one = taps(conv_one * half).transpose(1, 5, 0, 2, 3, 4)
    one = jnp.pad(one, ((0, 0), (0, 0), (0, WIN - 4), (0, 0), (0, 0), (0, 0)))
    one = one.reshape(4 * inputs * WIN, 4 * hidden)
    two = taps(conv_two * half).reshape(2, 2, 2, 2, 2, 2, hidden, hidden)
    two = two.transpose(0, 2, 1, 3, 7, 4, 5, 6).reshape(16 * hidden, 4 * hidden)
    three = jnp.pad(taps(conv_three), ((0, 0),) * 4 + ((0, 4 - outputs), (0, 0)))
    three = three.reshape(2, 2, 2, 2, 2, 2, 4, hidden).transpose(0, 2, 5, 4, 6, 1, 3, 7)
    three = three.reshape(64, 4 * hidden)
    low = jnp.tile(0.5 * bias_one, 4)[None]
    mid = jnp.tile(0.5 * bias_two, 4)[None]
    high = jnp.tile(jnp.pad(bias_three, (0, 4 - outputs)), 4)[:, None]
    return one, low, two, mid, three, high


def gate(value):
    return value + value * jnp.tanh(value)


def closure_kernel(
    depth_ref,
    features_ref,
    reach_ref,
    one_ref,
    low_ref,
    two_ref,
    mid_ref,
    three_ref,
    high_ref,
    split_ref,
    mask_ref,
    merge_ref,
    north_ref,
    spread_ref,
    first_ref,
    second_ref,
    out_ref,
    parts,
    hidden,
    shifted,
    top,
    stress,
):
    levels, rows3, cols = features_ref.shape
    rows_in = rows3 // 3
    rows_out = rows_in - 2 * HALO
    tiles = cols // LANES
    block_rows = rows_out // 2 + 1
    f32 = jnp.float32
    out_ref[...] = jnp.zeros_like(out_ref)
    parts[...] = jnp.zeros_like(parts)
    top[...] = jnp.zeros_like(top)
    stress[...] = jnp.zeros_like(stress)

    def window(ref, lead, col):
        at = lambda c: ref[lead + (slice(None), pl.ds(pl.multiple_of(c * LANES, LANES), LANES))]
        here = at(col)
        zero = jnp.zeros_like(here)
        before = jnp.where(col > 0, at(jnp.maximum(col - 1, 0)), zero)
        after = jnp.where(col < tiles - 1, at(jnp.minimum(col + 1, tiles - 1)), zero)
        return jnp.concatenate([before, here, after], axis=1)

    def unit(level, col):
        source = window(features_ref, (level,), col)
        pieces = jnp.dot(source, split_ref[...], preferred_element_type=f32)
        for s in range(4):
            parts[s, 0:rows3, :] = pieces[:, s * LANES : (s + 1) * LANES]
        for block in range(block_rows + 2):
            stack = jnp.concatenate(
                [
                    parts[s, c * rows_in + 2 * block : c * rows_in + 2 * block + WIN, :]
                    for s in range(4)
                    for c in range(3)
                ],
                axis=0,
            )
            rows = stack.T[0:PITCH].astype(jnp.bfloat16)
            value = jnp.dot(rows, one_ref[...], preferred_element_type=f32) + low_ref[...]
            value = gate(value)
            hidden[block * PITCH : (block + 1) * PITCH, :] = value.astype(jnp.bfloat16)
            shifted[block * PITCH : (block + 1) * PITCH, :] = pltpu.roll(
                value, PITCH - 1, 0
            ).astype(jnp.bfloat16)
        step = 6
        for block in range(0, block_rows + 1, step):
            count = min(step, block_rows + 1 - block)
            here = slice(block * PITCH, (block + count) * PITCH)
            below = slice((block + 1) * PITCH, (block + 1 + count) * PITCH)
            rows = jnp.concatenate(
                [hidden[here, :], shifted[here, :], hidden[below, :], shifted[below, :]], axis=1
            )
            value = jnp.dot(rows, two_ref[...], preferred_element_type=f32) + mid_ref[...]
            top[here, :] = gate(value).astype(jnp.bfloat16)
        earlier = None
        for block in range(block_rows + 1):
            rows = top[block * PITCH : block * PITCH + LANES, :]
            sums = lax.dot_general(
                three_ref[...], rows, (((1,), (1,)), ((), ())), preferred_element_type=f32
            )
            if earlier is not None:
                value = (
                    earlier[0:16]
                    + sums[32:48]
                    + pltpu.roll(earlier[16:32] + sums[48:64], LANES - 1, 1)
                    + high_ref[...]
                )
                stress[(block - 1) * 8 : block * 8, 0:LANES] = value[0:8]
                stress[(block - 1) * 8 : block * 8, LANES : 2 * LANES] = value[8:16]
            earlier = sums
        reach = window(reach_ref, (), col)
        active = jnp.where(reach > level.astype(f32), 1.0, 0.0)
        wide = jnp.dot(active.astype(jnp.bfloat16), mask_ref[...], preferred_element_type=f32)
        wide = jnp.dot(spread_ref[...], wide.astype(jnp.bfloat16), preferred_element_type=f32)
        masked = jnp.where(wide > 0.5, stress[...], 0.0).astype(jnp.bfloat16)
        natural = jnp.dot(masked, merge_ref[...], preferred_element_type=f32).astype(jnp.bfloat16)
        chosen = jnp.dot(second_ref[...], masked, preferred_element_type=f32).astype(jnp.bfloat16)
        push = jnp.dot(first_ref[...], natural, preferred_element_type=f32) + jnp.dot(
            chosen, north_ref[...], preferred_element_type=f32
        )
        own = active[HALO : HALO + rows_out, LANES : 2 * LANES]
        push = push * jnp.concatenate([own, own], axis=0)
        out_ref[level, :, pl.ds(pl.multiple_of(col * LANES, LANES), LANES)] = push.astype(jnp.bfloat16)

    def visit(index, carry):
        level, col = index // tiles, index % tiles

        @pl.when(level < depth_ref[col])
        def _():
            unit(level, col)

        return carry

    lax.fori_loop(0, levels * tiles, visit, 0)


def closure(depth, features, reach, weights, tables):
    levels, rows3, cols = features.shape
    rows_in = rows3 // 3
    rows_out = rows_in - 2 * HALO
    block_rows = rows_out // 2 + 1
    width = weights[2].shape[1]
    vmem = pl.BlockSpec(memory_space=pltpu.VMEM)
    operands = (features, reach) + tuple(weights) + tuple(tables)
    return pl.pallas_call(
        closure_kernel,
        out_shape=jax.ShapeDtypeStruct((levels, 2 * rows_out, cols), jnp.bfloat16),
        in_specs=[pl.BlockSpec(memory_space=pltpu.SMEM)] + [vmem] * len(operands),
        out_specs=vmem,
        scratch_shapes=[
            pltpu.VMEM((4, rows3 + WIN, LANES), jnp.float32),
            pltpu.VMEM(((block_rows + 2) * PITCH, width), jnp.bfloat16),
            pltpu.VMEM(((block_rows + 2) * PITCH, width), jnp.bfloat16),
            pltpu.VMEM(((block_rows + 1) * PITCH + LANES, width), jnp.bfloat16),
            pltpu.VMEM((tables[4].shape[0], 2 * LANES), jnp.float32),
        ],
        compiler_params=pltpu.CompilerParams(vmem_limit_bytes=48 * 1024 * 1024),
        name="closure",
    )(depth, *operands)


def body(
    velocity_u,
    velocity_v,
    tracer,
    land,
    tile_depth,
    conv_one,
    bias_one,
    conv_two,
    bias_two,
    conv_three,
    bias_three,
):
    levels_here, rows, cols = velocity_u.shape
    across = cols // rows
    group_index = lax.axis_index("group")
    tile_index = lax.axis_index("tile")
    group_count = lax.axis_size("group")
    tile_count = lax.axis_size("tile")
    total_rows = rows * tile_count
    share = rows // group_count
    edge = HALO + 1
    depth_grid = tile_depth.reshape(tile_count, across)
    my_depth = lax.dynamic_index_in_dim(depth_grid, tile_index, 0, keepdims=False)
    reach_here = jnp.where(land == 1, jnp.repeat(my_depth, rows)[None], 0).astype(jnp.float32)
    stacked = jnp.concatenate([velocity_u, velocity_v, tracer, reach_here[None]], axis=0)
    extended = extend_rows(stacked, edge)
    reach = extended[-1]
    fields = extended[:-1].reshape(3, levels_here, rows + 2 * edge, cols)
    fields = jnp.pad(fields, ((0, 0), (0, 0), (0, 0), (1, 1)))
    my_levels = (group_index * levels_here + jnp.arange(levels_here, dtype=jnp.int32)).astype(jnp.float32)
    active = (my_levels[:, None, None] < reach[None, 1:-1]).astype(jnp.float32)
    places = (tile_index * rows - HALO + jnp.arange(rows + 2 * HALO, dtype=jnp.int32)).astype(jnp.float32)
    coriolis = (coriolis_base + coriolis_slope * (places + 0.5) / total_rows)[:, None]
    east, north, new_tracer = advance(fields[0], fields[1], fields[2], active, coriolis)
    features = (jnp.stack([east, north, new_tracer], axis=1) * active[:, None]).astype(jnp.bfloat16)
    shares = jnp.stack(
        [features[:, :, q * share : (q + 1) * share + 2 * HALO] for q in range(group_count)]
    )
    shares = shares.reshape(group_count, levels_here, 3 * (share + 2 * HALO), cols)
    arriving = lax.all_to_all(shares, "group", split_axis=0, concat_axis=0, tiled=True)
    arriving = arriving.reshape((group_count * levels_here,) + arriving.shape[2:])
    my_reach = lax.dynamic_slice_in_dim(reach, group_index * share + 1, share + 2 * HALO, 0)
    weights = arranged_weights(conv_one, bias_one, conv_two, bias_two, conv_three, bias_three)
    push = closure(my_depth, arriving, my_reach, weights, operators(share))
    push = push.reshape(group_count, levels_here, 2, share, cols)
    landed = lax.all_to_all(push, "group", split_axis=0, concat_axis=0, tiled=True)
    added = landed.transpose(2, 1, 0, 3, 4).reshape(2, levels_here, rows, cols).astype(jnp.float32)
    inner = slice(HALO, HALO + rows)
    return (east[:, inner] + added[0], north[:, inner] + added[1], new_tracer[:, inner])


def solution(mesh):
    field = P("group", "tile", None)
    in_specs = (field, field, field, P("tile", None)) + (P(),) * 7
    return jax.shard_map(
        body, mesh=mesh, in_specs=in_specs, out_specs=(field,) * 3, check_vma=False
    )
```

```python
import jax
import jax.numpy as jnp
import numpy as np
from jax import lax
from jax.experimental import pallas as pl
from jax.experimental.pallas import tpu as pltpu
from jax.sharding import PartitionSpec as P

time_step = 0.1
viscosity = 0.5
diffusivity = 0.5
eddy_gain = 0.5
coriolis_base = 0.2
coriolis_slope = 0.6

LANES = 128
STRIPS = 16
HALO = 4
PAD = 16
LEAD = 8


def taps(kernel):
    return jnp.stack(
        [
            jnp.stack(
                [
                    jnp.pad(kernel.transpose(2, 3, 0, 1), ((p, 1 - p), (par, 1 - par), (0, 0), (0, 0)))
                    for par in range(2)
                ],
                axis=2,
            )
            for p in range(2)
        ],
        axis=2,
    )


def arranged_weights(conv_one, bias_one, conv_two, bias_two, conv_three, bias_three):
    hidden, inputs = conv_one.shape[:2]
    outputs = conv_three.shape[0]
    half = jnp.asarray(0.5, jnp.bfloat16)
    one = taps(conv_one * half).transpose(5, 1, 0, 2, 3, 4).reshape(16 * inputs, 4 * hidden)
    one = jnp.pad(one, ((0, LANES - one.shape[0]), (0, 0)))
    two = (conv_two * half).transpose(2, 3, 1, 0)
    two = jnp.concatenate(
        [jnp.pad(two, ((0, 0), (par, 1 - par), (0, 0), (0, 0))) for par in range(2)], axis=3
    )
    three = jnp.pad(taps(conv_three), ((0, 0),) * 4 + ((0, 4 - outputs), (0, 0)))
    three = three.reshape(2, 2, 2, 2, 2, 2, 4, hidden).transpose(0, 2, 5, 4, 6, 1, 3, 7)
    three = three.reshape(64, 4 * hidden)
    low = jnp.tile(0.5 * bias_one, 4)[None]
    mid = jnp.tile(0.5 * bias_two, 4)[None]
    high = jnp.tile(jnp.pad(bias_three, (0, 4 - outputs)), 4)[:, None]
    return one, low, two, mid, three, high


def tables(cols):
    w, lane = np.arange(3 * LANES), np.arange(LANES)
    split = np.concatenate([w[:, None] == (2 * lane - 3 + s + LANES)[None] for s in range(4)], axis=1)
    groups = cols // 2 // STRIPS
    index = np.arange(cols)
    par, rest = index // (cols // 2), index % (cols // 2)
    place = 2 * (groups * (rest % STRIPS) + rest // STRIPS) + par
    merge = place[:, None] == index[None]
    return [jnp.asarray(np.asarray(t, np.float32), jnp.bfloat16) for t in (split, merge)]


def gate(value):
    return value + value * jnp.tanh(value)


def step_kernel(
    depth_ref,
    where_ref,
    east_ref,
    north_ref,
    tracer_ref,
    land_ref,
    upper_ref,
    lower_ref,
    one_ref,
    low_ref,
    taps_ref,
    mid_ref,
    three_ref,
    high_ref,
    split_ref,
    merge_ref,
    out_east,
    out_north,
    out_tracer,
    fields,
    sheet,
    depths,
    parts,
    turned,
    ready,
    two,
    hidden,
    top,
    sums,
    stress,
    natural,
):
    levels_here, rows, cols = east_ref.shape
    edge = upper_ref.shape[1]
    f32, bf16 = jnp.float32, jnp.bfloat16
    groups = cols // 2 // STRIPS
    half = cols // 2
    rows_one, rows_two = (groups + 2) * STRIPS, (groups + 1) * STRIPS
    pitch = sheet.shape[0] // 3
    windows = -(-(half + 2) // LANES)
    turns = (rows + 4) // 4
    lane = lax.broadcasted_iota(jnp.int32, (8, cols), 1)
    sub = lax.broadcasted_iota(jnp.int32, (8, LANES), 0)

    channels = taps_ref.shape[2]
    for k in range(16):
        by, bx, py, px = k // 8, k // 4 % 2, k // 2 % 2, k % 2
        for p in range(2):
            tap = 2 * by + py - p
            at = (slice(k * channels, (k + 1) * channels), slice(p * LANES, (p + 1) * LANES))
            two[at] = taps_ref[tap, 2 * bx + px] if 0 <= tap < 3 else jnp.zeros((channels, LANES), bf16)
    parts[...] = jnp.zeros_like(parts)
    turned[...] = jnp.zeros_like(turned)
    sheet[...] = jnp.zeros_like(sheet)
    sums[...] = jnp.zeros_like(sums)
    top[...] = jnp.zeros_like(top)

    for tile in range(cols // LANES):
        depths[:, tile * LANES : (tile + 1) * LANES] = jnp.full(
            (8, LANES), depth_ref[tile * LANES // rows], jnp.int32
        ).astype(f32)

    def frame(slot, source, inner):
        fields[slot, 0:PAD, :] = jnp.zeros((PAD, cols), f32)
        fields[slot, PAD + rows :, :] = jnp.zeros((PAD, cols), f32)
        fields[slot, PAD - edge : PAD, :] = upper_ref[source]
        fields[slot, PAD + rows : PAD + rows + edge, :] = lower_ref[source]
        for r in range(0, rows, 8):
            fields[slot, PAD + r : PAD + r + 8, :] = inner(r)

    frame(3, 3 * levels_here, lambda r: jnp.where(land_ref[r : r + 8, :] == 1, depths[...], 0.0))

    def sideways(value):
        left = jnp.where(lane > 0, pltpu.roll(value, 1, 1), 0.0)
        right = jnp.where(lane < cols - 1, pltpu.roll(value, cols - 1, 1), 0.0)
        return left, right

    def wet(number, at):
        return jnp.where(number < fields[3, at : at + 8, :], 1.0, 0.0)

    def advance(level, number):
        for f, ref in enumerate((east_ref, north_ref, tracer_ref)):
            frame(f, f * levels_here + level, lambda r: ref[level, r : r + 8, :])
        saved = [None] * 3
        for start in range(-8, rows + 8, 8):
            at = start + PAD

            def around(slot):
                here = fields[slot, at : at + 8, :]
                return (here, fields[slot, at - 1 : at + 7, :], fields[slot, at + 1 : at + 9, :]) + sideways(here)

            def curvature(a):
                return a[2] + a[1] + a[4] + a[3] - 4.0 * a[0]

            east, north, tracer = around(0), around(1), around(2)
            active = wet(number, at)
            row = where_ref[1] + start + lax.broadcasted_iota(jnp.int32, (8, cols), 0)
            coriolis = coriolis_base + coriolis_slope * (row.astype(f32) + 0.5) / where_ref[2].astype(f32)
            grad_east = 0.5 * (tracer[2] - tracer[1])
            grad_north = 0.5 * (tracer[4] - tracer[3])
            rate = time_step * active
            news = (
                east[0] + rate * (coriolis * north[0] - grad_east + viscosity * curvature(east)),
                north[0] + rate * (-coriolis * east[0] - grad_north + viscosity * curvature(north)),
                tracer[0]
                + rate * (-(east[0] * grad_east + north[0] * grad_north) + diffusivity * curvature(tracer)),
            )
            for f, (new, out) in enumerate(zip(news, (out_east, out_north, out_tracer), strict=True)):
                if 0 <= start < rows:
                    out[level, start : start + 8, :] = new
                new = new * active
                first, last = max(start, -HALO), min(start + 8, rows + HALO)
                sheet[f * pitch + first + HALO : f * pitch + last + HALO, LANES : LANES + cols] = new[
                    first - start : last - start
                ]

    def split_columns():
        for m in range(windows):
            source = sheet[:, 2 * m * LANES : (2 * m + 3) * LANES].astype(bf16)
            pieces = jnp.dot(source, split_ref[...], preferred_element_type=f32)
            for s in range(4):
                parts[s, m, LEAD : LEAD + 3 * pitch, :] = pieces[:, s * LANES : (s + 1) * LANES]

    def prepare(slot, base, offset):
        for m in range(windows):
            at = lambda s, first: parts[s, m, pl.ds(base + first, 8), :]
            stack = jnp.concatenate(
                [
                    jnp.where(
                        sub < 4,
                        at(s, LEAD + c * pitch + offset),
                        at(s + 1, LEAD + c * pitch + offset - 4),
                    )
                    for c in range(3)
                    for s in (0, 2)
                ],
                axis=0,
            )
            turned[slot, m * LANES : (m + 1) * LANES, 0:48] = stack.T
        for t in range(groups + 2):
            ready[slot, t * STRIPS : (t + 1) * STRIPS, :] = turned[slot, pl.ds(t, STRIPS, groups), :].astype(bf16)

    def layer_one(slot, target):
        value = jnp.dot(ready[slot], one_ref[...], preferred_element_type=f32)
        hidden[target] = gate(value + low_ref[...]).astype(bf16)

    def layer_two(slot):
        gathered = jnp.concatenate(
            [hidden[slot + by, bx * STRIPS : bx * STRIPS + rows_two, :] for by in range(2) for bx in range(2)],
            axis=1,
        )
        value = jnp.dot(gathered, two[...], preferred_element_type=f32)
        top[slot, 0:rows_two, :] = gate(value + mid_ref[...]).astype(bf16)

    def layer_three(slot, base, offset):
        new = lax.dot_general(
            three_ref[...], top[slot], (((1,), (1,)), ((), ())), preferred_element_type=f32
        )
        old = sums[...]
        wide = pltpu.roll(old[16:32] + new[48:64], new.shape[1] - STRIPS, 1)
        value = old[0:16, 0:half] + new[32:48, 0:half] + wide[:, 0:half] + high_ref[...]
        stress[pl.ds(base + offset, 8), 0:half] = value[0:8]
        stress[pl.ds(base + offset, 8), half:cols] = value[8:16]
        sums[...] = new

    def finish(level, number):
        merged = jnp.dot(stress[24:, :].astype(bf16), merge_ref[...], preferred_element_type=f32)
        for tile in range(cols // LANES):
            natural[tile] = merged[:, tile * LANES : (tile + 1) * LANES]

        def field(start, shift, comp):
            at = pl.ds(4 * (start + 1 + shift) + comp, 8, 4)
            value = jnp.concatenate([natural[tile, at, :] for tile in range(cols // LANES)], axis=1)
            return value * wet(number, start + PAD + shift)

        for start in range(0, rows, 8):
            rate = eddy_gain * wet(number, start + PAD)
            east_left, east_right = sideways(field(start, 0, 1))
            north_left, north_right = sideways(field(start, 0, 2))
            push_east = 0.5 * (field(start, 1, 0) - field(start, -1, 0)) + 0.5 * (east_right - east_left)
            push_north = 0.5 * (field(start, 1, 1) - field(start, -1, 1)) + 0.5 * (north_right - north_left)
            out_east[level, start : start + 8, :] += rate * push_east
            out_north[level, start : start + 8, :] += rate * push_north

    for level in range(levels_here):
        number = (where_ref[0] + level).astype(f32)
        advance(level, number)
        split_columns()
        for slot in range(3):
            prepare(slot % 2, 0, 2 * slot)
            layer_one(slot % 2, slot)
        prepare(0, 0, 6)
        prepare(1, 0, 8)

        def turn(k, carry):
            layer_three(0, pl.multiple_of(16 * k, 16), 0)
            layer_three(1, pl.multiple_of(16 * k, 16), 8)
            layer_two(0)
            layer_two(1)
            hidden[0] = hidden[2]
            layer_one(0, 1)
            layer_one(1, 2)
            prepare(0, 4 * k, 10)
            prepare(1, 4 * k, 12)
            return carry

        lax.fori_loop(0, turns, turn, 0)
        layer_three(0, 16 * turns, 0)
        layer_three(1, 16 * turns, 8)
        finish(level, number)


def ocean_step(depth, where, fields, land, upper, lower, weights):
    levels_here, rows, cols = fields[0].shape
    width = weights[1].shape[1]
    half = cols // 2
    groups = half // STRIPS
    windows = -(-(half + 2) // LANES)
    turns = (rows + 4) // 4
    pitch = rows + 4 * HALO
    vmem = pl.BlockSpec(memory_space=pltpu.VMEM)
    smem = pl.BlockSpec(memory_space=pltpu.SMEM)
    operands = tuple(fields) + (land, upper, lower) + tuple(weights) + tuple(tables(cols))
    field = jax.ShapeDtypeStruct(fields[0].shape, jnp.float32)
    top_rows = -(-(groups + 1) * STRIPS // LANES) * LANES
    return pl.pallas_call(
        step_kernel,
        out_shape=(field,) * 3,
        in_specs=[smem, smem] + [vmem] * len(operands),
        out_specs=(vmem,) * 3,
        scratch_shapes=[
            pltpu.VMEM((4, rows + 2 * PAD, cols), jnp.float32),
            pltpu.VMEM((3 * pitch, (2 * windows + 1) * LANES), jnp.float32),
            pltpu.VMEM((8, cols), jnp.float32),
            pltpu.VMEM((4, windows, LEAD + 3 * pitch + 24, LANES), jnp.float32),
            pltpu.VMEM((2, windows * LANES, LANES), jnp.float32),
            pltpu.VMEM((2, (groups + 2) * STRIPS, LANES), jnp.bfloat16),
            pltpu.VMEM((4 * width, width), jnp.bfloat16),
            pltpu.VMEM((3, (groups + 2) * STRIPS, width), jnp.bfloat16),
            pltpu.VMEM((2, top_rows, width), jnp.bfloat16),
            pltpu.VMEM((64, top_rows), jnp.float32),
            pltpu.VMEM((16 * (turns + 1), cols), jnp.float32),
            pltpu.VMEM((cols // LANES, 16 * (turns + 1) - 24, LANES), jnp.float32),
        ],
        compiler_params=pltpu.CompilerParams(vmem_limit_bytes=60 * 1024 * 1024),
        name="step",
    )(depth, where, *operands)


def body(
    velocity_u,
    velocity_v,
    tracer,
    land,
    tile_depth,
    conv_one,
    bias_one,
    conv_two,
    bias_two,
    conv_three,
    bias_three,
):
    levels_here, rows, cols = velocity_u.shape
    across = cols // rows
    group_index = lax.axis_index("group")
    tile_index = lax.axis_index("tile")
    tile_count = lax.axis_size("tile")
    edge = HALO + 1
    depth_grid = tile_depth.reshape(tile_count, across)
    my_depth = lax.dynamic_index_in_dim(depth_grid, tile_index, 0, keepdims=False)
    column_depth = jnp.repeat(my_depth, rows)[None]

    def border(at):
        reach = jnp.where(land[at] == 1, column_depth, 0).astype(jnp.float32)
        return jnp.concatenate([velocity_u[:, at], velocity_v[:, at], tracer[:, at], reach[None]], axis=0)

    forward = [(i, i + 1) for i in range(tile_count - 1)]
    backward = [(target, source) for source, target in forward]
    upper = lax.ppermute(border(slice(rows - edge, rows)), "tile", forward)
    lower = lax.ppermute(border(slice(0, edge)), "tile", backward)
    where = jnp.stack(
        [
            jnp.asarray(group_index * levels_here, jnp.int32),
            jnp.asarray(tile_index * rows, jnp.int32),
            jnp.asarray(tile_count * rows, jnp.int32),
        ]
    )
    weights = arranged_weights(conv_one, bias_one, conv_two, bias_two, conv_three, bias_three)
    return ocean_step(my_depth, where, (velocity_u, velocity_v, tracer), land, upper, lower, weights)


def solution(mesh):
    field = P("group", "tile", None)
    in_specs = (field, field, field, P("tile", None)) + (P(),) * 7
    return jax.shard_map(
        body, mesh=mesh, in_specs=in_specs, out_specs=(field,) * 3, check_vma=False
    )
```

```python
import jax
import jax.numpy as jnp
import numpy as np
from jax import lax
from jax.experimental import pallas as pl
from jax.experimental.pallas import tpu as pltpu
from jax.sharding import PartitionSpec as P

time_step = 0.1
viscosity = 0.5
diffusivity = 0.5
eddy_gain = 0.5
coriolis_base = 0.2
coriolis_slope = 0.6

LANES = 128
STRIPS = 16
HALO = 4
PAD = 16
LEAD = 8
TURN = 6


def taps(kernel):
    return jnp.stack(
        [
            jnp.stack(
                [
                    jnp.pad(kernel.transpose(2, 3, 0, 1), ((p, 1 - p), (par, 1 - par), (0, 0), (0, 0)))
                    for par in range(2)
                ],
                axis=2,
            )
            for p in range(2)
        ],
        axis=2,
    )


def arranged_weights(conv_one, bias_one, conv_two, bias_two, conv_three, bias_three):
    hidden, inputs = conv_one.shape[:2]
    outputs = conv_three.shape[0]
    half = jnp.asarray(0.5, jnp.bfloat16)
    one = taps(conv_one * half).transpose(5, 1, 0, 2, 3, 4).reshape(16 * inputs, 4 * hidden)
    rest, pieces = jnp.tile(0.5 * bias_one, 4)[None], []
    for _ in range(3):
        pieces.append(lax.reduce_precision(rest, 8, 7))
        rest = rest - pieces[-1]
    one = jnp.concatenate([one] + [piece.astype(jnp.bfloat16) for piece in pieces], axis=0)
    one = jnp.pad(one, ((0, LANES - one.shape[0]), (0, 0)))
    two = (conv_two * half).transpose(2, 3, 1, 0)
    two = jnp.concatenate(
        [jnp.pad(two, ((0, 0), (par, 1 - par), (0, 0), (0, 0))) for par in range(2)], axis=3
    )
    three = jnp.pad(taps(conv_three), ((0, 0),) * 4 + ((0, 4 - outputs), (0, 0)))
    three = three.reshape(2, 2, 2, 2, 2, 2, 4, hidden).transpose(0, 2, 5, 4, 6, 1, 3, 7)
    three = three.reshape(64, 4 * hidden)
    mid = jnp.tile(0.5 * bias_two, 4)[None]
    high = jnp.tile(jnp.pad(bias_three, (0, 4 - outputs)), 4)[:, None]
    return one, two, mid, three, high


def tables(cols):
    w, lane = np.arange(3 * LANES), np.arange(LANES)
    split = np.concatenate([w[:, None] == (2 * lane - 3 + s + LANES)[None] for s in range(4)], axis=1)
    groups = cols // 2 // STRIPS
    index = np.arange(cols)
    par, rest = index // (cols // 2), index % (cols // 2)
    place = 2 * (groups * (rest % STRIPS) + rest // STRIPS) + par
    merge = place[:, None] == index[None]
    return [jnp.asarray(np.asarray(t, np.float32), jnp.bfloat16) for t in (split, merge)]


def gate(value):
    return value + value * jnp.tanh(value)


def step_kernel(
    depth_ref,
    where_ref,
    east_ref,
    north_ref,
    tracer_ref,
    land_ref,
    upper_ref,
    lower_ref,
    one_ref,
    taps_ref,
    mid_ref,
    three_ref,
    high_ref,
    split_ref,
    merge_ref,
    out_east,
    out_north,
    out_tracer,
    fields,
    sheet,
    depths,
    parts,
    turned,
    ready,
    two,
    hidden,
    top,
    sums,
    stress,
    natural,
):
    levels_here, rows, cols = east_ref.shape
    edge = upper_ref.shape[1]
    f32, bf16 = jnp.float32, jnp.bfloat16
    groups = cols // 2 // STRIPS
    half = cols // 2
    rows_one, rows_two = (groups + 2) * STRIPS, (groups + 1) * STRIPS
    pitch = sheet.shape[0] // 3
    windows = -(-(half + 2) // LANES)
    turns = (rows // 2 + 2) // TURN
    strip = groups + 3
    lane = lax.broadcasted_iota(jnp.int32, (8, cols), 1)
    sub = lax.broadcasted_iota(jnp.int32, (8, LANES), 0)

    channels = taps_ref.shape[2]
    for k in range(16):
        by, bx, py, px = k // 8, k // 4 % 2, k // 2 % 2, k % 2
        for p in range(2):
            tap = 2 * by + py - p
            at = (slice(k * channels, (k + 1) * channels), slice(p * LANES, (p + 1) * LANES))
            two[at] = taps_ref[tap, 2 * bx + px] if 0 <= tap < 3 else jnp.zeros((channels, LANES), bf16)
    parts[...] = jnp.zeros_like(parts)
    columns = lax.broadcasted_iota(jnp.int32, turned.shape, 2)
    turned[...] = jnp.where((columns >= 48) & (columns < 51), 1.0, 0.0)
    sheet[...] = jnp.zeros_like(sheet)
    sums[...] = jnp.zeros_like(sums)
    top[...] = jnp.zeros_like(top)

    for tile in range(cols // LANES):
        depths[:, tile * LANES : (tile + 1) * LANES] = jnp.full(
            (8, LANES), depth_ref[tile * LANES // rows], jnp.int32
        ).astype(f32)

    def frame(slot, source, inner):
        fields[slot, 0:PAD, :] = jnp.zeros((PAD, cols), f32)
        fields[slot, PAD + rows :, :] = jnp.zeros((PAD, cols), f32)
        fields[slot, PAD - edge : PAD, :] = upper_ref[source]
        fields[slot, PAD + rows : PAD + rows + edge, :] = lower_ref[source]
        for r in range(0, rows, 8):
            fields[slot, PAD + r : PAD + r + 8, :] = inner(r)

    frame(3, 3 * levels_here, lambda r: jnp.where(land_ref[r : r + 8, :] == 1, depths[...], 0.0))

    def sideways(value):
        left = jnp.where(lane > 0, pltpu.roll(value, 1, 1), 0.0)
        right = jnp.where(lane < cols - 1, pltpu.roll(value, cols - 1, 1), 0.0)
        return left, right

    def wet(number, at):
        return jnp.where(number < fields[3, at : at + 8, :], 1.0, 0.0)

    def advance(level, number):
        for f, ref in enumerate((east_ref, north_ref, tracer_ref)):
            frame(f, f * levels_here + level, lambda r: ref[level, r : r + 8, :])
        saved = [None] * 3
        for start in range(-8, rows + 8, 8):
            at = start + PAD

            def around(slot):
                here = fields[slot, at : at + 8, :]
                return (here, fields[slot, at - 1 : at + 7, :], fields[slot, at + 1 : at + 9, :]) + sideways(here)

            def curvature(a):
                return a[2] + a[1] + a[4] + a[3] - 4.0 * a[0]

            east, north, tracer = around(0), around(1), around(2)
            active = wet(number, at)
            row = where_ref[1] + start + lax.broadcasted_iota(jnp.int32, (8, cols), 0)
            coriolis = coriolis_base + coriolis_slope * (row.astype(f32) + 0.5) / where_ref[2].astype(f32)
            grad_east = 0.5 * (tracer[2] - tracer[1])
            grad_north = 0.5 * (tracer[4] - tracer[3])
            rate = time_step * active
            news = (
                east[0] + rate * (coriolis * north[0] - grad_east + viscosity * curvature(east)),
                north[0] + rate * (-coriolis * east[0] - grad_north + viscosity * curvature(north)),
                tracer[0]
                + rate * (-(east[0] * grad_east + north[0] * grad_north) + diffusivity * curvature(tracer)),
            )
            for f, (new, out) in enumerate(zip(news, (out_east, out_north, out_tracer), strict=True)):
                if 0 <= start < rows:
                    out[level, start : start + 8, :] = new
                new = new * active
                first, last = max(start, -HALO), min(start + 8, rows + HALO)
                sheet[f * pitch + first + HALO : f * pitch + last + HALO, LANES : LANES + cols] = new[
                    first - start : last - start
                ]

    def split_columns():
        for m in range(windows):
            source = sheet[:, 2 * m * LANES : (2 * m + 3) * LANES].astype(bf16)
            pieces = jnp.dot(source, split_ref[...], preferred_element_type=f32)
            for s in range(4):
                parts[s, m, LEAD : LEAD + 3 * pitch, :] = pieces[:, s * LANES : (s + 1) * LANES]

    def prepare(slot, base, offset):
        flipped, twin = [], slot % 2
        for m in range(windows):
            at = lambda s, first: parts[s, m, pl.ds(base + first, 8), :]
            stack = jnp.concatenate(
                [
                    jnp.where(
                        sub < 4,
                        at(s, LEAD + c * pitch + offset),
                        at(s + 1, LEAD + c * pitch + offset - 4),
                    )
                    for c in range(3)
                    for s in (0, 2)
                ],
                axis=0,
            )
            flipped.append(stack.T)
        flipped = jnp.concatenate(flipped, axis=0)
        for s in range(STRIPS):
            turned[twin, s * strip : s * strip + groups + 8, 0:48] = flipped[s * groups : (s + 1) * groups + 8]
        for t in range(groups + 2):
            ready[slot, t * STRIPS : (t + 1) * STRIPS, :] = turned[twin, pl.ds(t, STRIPS, strip), :].astype(bf16)

    def layer_one(slot, target):
        value = jnp.dot(ready[slot], one_ref[...], preferred_element_type=f32)
        hidden[target] = gate(value).astype(bf16)

    def layer_two(slot):
        gathered = jnp.concatenate(
            [hidden[slot + by, bx * STRIPS : bx * STRIPS + rows_two, :] for by in range(2) for bx in range(2)],
            axis=1,
        )
        value = jnp.dot(gathered, two[...], preferred_element_type=f32)
        top[slot, 0:rows_two, :] = gate(value + mid_ref[...]).astype(bf16)

    def layer_three(slot, base, offset):
        new = lax.dot_general(
            three_ref[...], top[slot], (((1,), (1,)), ((), ())), preferred_element_type=f32
        )
        old = sums[...]
        wide = old[16:32, STRIPS : STRIPS + half] + new[48:64, STRIPS : STRIPS + half]
        value = old[0:16, 0:half] + new[32:48, 0:half] + wide + high_ref[...]
        stress[pl.ds(base + offset, 8), 0:half] = value[0:8]
        stress[pl.ds(base + offset, 8), half:cols] = value[8:16]
        sums[...] = new

    def finish(level, number):
        merged = jnp.dot(stress[8 * (TURN + 1) :, :].astype(bf16), merge_ref[...], preferred_element_type=f32)
        for tile in range(cols // LANES):
            natural[tile] = merged[:, tile * LANES : (tile + 1) * LANES]

        def field(start, shift, comp):
            at = pl.ds(4 * (start + 1 + shift) + comp, 8, 4)
            value = jnp.concatenate([natural[tile, at, :] for tile in range(cols // LANES)], axis=1)
            return value * wet(number, start + PAD + shift)

        for start in range(0, rows, 8):
            rate = eddy_gain * wet(number, start + PAD)
            east_left, east_right = sideways(field(start, 0, 1))
            north_left, north_right = sideways(field(start, 0, 2))
            push_east = 0.5 * (field(start, 1, 0) - field(start, -1, 0)) + 0.5 * (east_right - east_left)
            push_north = 0.5 * (field(start, 1, 1) - field(start, -1, 1)) + 0.5 * (north_right - north_left)
            out_east[level, start : start + 8, :] += rate * push_east
            out_north[level, start : start + 8, :] += rate * push_north

    for level in range(levels_here):
        number = (where_ref[0] + level).astype(f32)
        advance(level, number)
        split_columns()
        for slot in range(TURN + 1):
            prepare(slot % TURN, 0, 2 * slot)
            layer_one(slot % TURN, slot)
        for slot in range(TURN):
            prepare(slot, 0, 2 * (TURN + 1 + slot))

        def turn(k, carry):
            at = pl.multiple_of(8 * TURN * k, 16)
            base = 2 * TURN * k
            for i in range(TURN):
                layer_three(i, at, 8 * i)
                layer_two(i)
                if i:
                    layer_one(i - 1, i)
                    prepare(i - 1, base, 2 * (2 * TURN + i))
            hidden[0] = hidden[TURN]
            layer_one(TURN - 1, TURN)
            prepare(TURN - 1, base, 6 * TURN)
            return carry

        lax.fori_loop(0, turns, turn, 0)
        for i in range(TURN):
            layer_three(i, 8 * TURN * turns, 8 * i)
        finish(level, number)


def ocean_step(depth, where, fields, land, upper, lower, weights):
    levels_here, rows, cols = fields[0].shape
    width = weights[0].shape[1]
    half = cols // 2
    groups = half // STRIPS
    windows = -(-(half + 2) // LANES)
    turns = (rows // 2 + 2) // TURN
    pitch = rows + 4 * HALO
    vmem = pl.BlockSpec(memory_space=pltpu.VMEM)
    smem = pl.BlockSpec(memory_space=pltpu.SMEM)
    operands = tuple(fields) + (land, upper, lower) + tuple(weights) + tuple(tables(cols))
    field = jax.ShapeDtypeStruct(fields[0].shape, jnp.float32)
    top_rows = (groups + 1) * STRIPS
    stress_rows = 8 * TURN * (turns + 1)
    return pl.pallas_call(
        step_kernel,
        out_shape=(field,) * 3,
        in_specs=[smem, smem] + [vmem] * len(operands),
        out_specs=(vmem,) * 3,
        scratch_shapes=[
            pltpu.VMEM((4, rows + 2 * PAD, cols), jnp.float32),
            pltpu.VMEM((3 * pitch, (2 * windows + 1) * LANES), jnp.float32),
            pltpu.VMEM((8, cols), jnp.float32),
            pltpu.VMEM((4, windows, LEAD + 3 * pitch + 8 * TURN, LANES), jnp.float32),
            pltpu.VMEM((2, STRIPS * (groups + 3) + 8, LANES), jnp.float32),
            pltpu.VMEM((TURN, (groups + 2) * STRIPS, LANES), jnp.bfloat16),
            pltpu.VMEM((4 * width, width), jnp.bfloat16),
            pltpu.VMEM((TURN + 1, (groups + 2) * STRIPS, width), jnp.bfloat16),
            pltpu.VMEM((TURN, top_rows, width), jnp.bfloat16),
            pltpu.VMEM((64, top_rows), jnp.float32),
            pltpu.VMEM((stress_rows, cols), jnp.float32),
            pltpu.VMEM((cols // LANES, stress_rows - 8 * (TURN + 1), LANES), jnp.float32),
        ],
        compiler_params=pltpu.CompilerParams(vmem_limit_bytes=40 * 1024 * 1024),
        name="step",
    )(depth, where, *operands)


def body(
    velocity_u,
    velocity_v,
    tracer,
    land,
    tile_depth,
    conv_one,
    bias_one,
    conv_two,
    bias_two,
    conv_three,
    bias_three,
):
    levels_here, rows, cols = velocity_u.shape
    across = cols // rows
    group_index = lax.axis_index("group")
    tile_index = lax.axis_index("tile")
    tile_count = lax.axis_size("tile")
    edge = HALO + 1
    depth_grid = tile_depth.reshape(tile_count, across)
    my_depth = lax.dynamic_index_in_dim(depth_grid, tile_index, 0, keepdims=False)
    column_depth = jnp.repeat(my_depth, rows)[None]

    def border(at):
        reach = jnp.where(land[at] == 1, column_depth, 0).astype(jnp.float32)
        return jnp.concatenate([velocity_u[:, at], velocity_v[:, at], tracer[:, at], reach[None]], axis=0)

    forward = [(i, i + 1) for i in range(tile_count - 1)]
    backward = [(target, source) for source, target in forward]
    upper = lax.ppermute(border(slice(rows - edge, rows)), "tile", forward)
    lower = lax.ppermute(border(slice(0, edge)), "tile", backward)
    where = jnp.stack(
        [
            jnp.asarray(group_index * levels_here, jnp.int32),
            jnp.asarray(tile_index * rows, jnp.int32),
            jnp.asarray(tile_count * rows, jnp.int32),
        ]
    )
    weights = arranged_weights(conv_one, bias_one, conv_two, bias_two, conv_three, bias_three)
    return ocean_step(my_depth, where, (velocity_u, velocity_v, tracer), land, upper, lower, weights)


def solution(mesh):
    field = P("group", "tile", None)
    in_specs = (field, field, field, P("tile", None)) + (P(),) * 7
    return jax.shard_map(
        body, mesh=mesh, in_specs=in_specs, out_specs=(field,) * 3, check_vma=False
    )
```

```python
import jax
import jax.numpy as jnp
from jax import lax
from jax.experimental import pallas as pl
from jax.experimental.pallas import tpu as pltpu
from jax.sharding import PartitionSpec as P

time_step = 0.1
viscosity = 0.5
diffusivity = 0.5
eddy_gain = 0.5
coriolis_base = 0.2
coriolis_slope = 0.6

LANES = 128
STRIPS = 16
HALO = 4
PAD = 16
LEAD = 8
EDGE = 8
TURN = 6


def gate(value):
    return value + value * jnp.tanh(value)


def border_kernel(depth_ref, east_ref, north_ref, tracer_ref, land_ref, first_ref, last_ref, shore, sems):
    levels_here, rows, cols = east_ref.shape
    depth = first_ref.shape[1]
    across = cols // rows
    tile_index = lax.axis_index("tile")
    copies = []
    for side, (target, start) in enumerate(((first_ref, 0), (last_ref, rows - depth))):
        at = pl.ds(start, depth)
        for f, ref in enumerate((east_ref, north_ref, tracer_ref)):
            for level in range(levels_here):
                slot = f * levels_here + level
                copies.append(pltpu.make_async_copy(ref.at[level, at], target.at[slot], sems.at[side, slot]))
        copies.append(pltpu.make_async_copy(land_ref.at[at], shore.at[side], sems.at[side, 3 * levels_here]))
    for copy in copies:
        copy.start()
    for copy in copies:
        copy.wait()
    for side, target in enumerate((first_ref, last_ref)):
        for tile in range(across):
            at = slice(tile * rows, (tile + 1) * rows)
            value = jnp.full((depth, rows), depth_ref[tile_index * across + tile], jnp.int32)
            target[3 * levels_here, :, at] = jnp.where(shore[side, :, at] == 1, value, 0).astype(jnp.float32)


def borders(tile_depth, fields, land, depth):
    levels_here, _, cols = fields[0].shape
    count = 3 * levels_here + 1
    edge = jax.ShapeDtypeStruct((count, depth, cols), jnp.float32)
    far = pl.BlockSpec(memory_space=pltpu.HBM)
    vmem = pl.BlockSpec(memory_space=pltpu.VMEM)
    return pl.pallas_call(
        border_kernel,
        out_shape=(edge, edge),
        in_specs=[pl.BlockSpec(memory_space=pltpu.SMEM)] + [far] * 4,
        out_specs=(vmem, vmem),
        scratch_shapes=[pltpu.VMEM((2, depth, cols), jnp.int32), pltpu.SemaphoreType.DMA((2, count))],
        compiler_params=pltpu.CompilerParams(vmem_limit_bytes=62 * 1024 * 1024),
        name="borders",
    )(tile_depth, *fields, land)


def step_kernel(
    depth_ref,
    high_ref,
    east_ref,
    north_ref,
    tracer_ref,
    land_ref,
    upper_ref,
    lower_ref,
    one_ref,
    low_ref,
    two_ref,
    mid_ref,
    three_ref,
    out_east,
    out_north,
    out_tracer,
    fields,
    shore,
    merge,
    split,
    one,
    three,
    rough,
    high,
    mid,
    sheet,
    parts,
    turned,
    ready,
    two,
    hidden,
    top,
    sums,
    stress,
    natural,
    sems,
):
    levels_here, rows, cols = east_ref.shape
    edge = upper_ref.shape[1]
    across = cols // rows
    f32, bf16 = jnp.float32, jnp.bfloat16
    groups = cols // 2 // STRIPS
    half = cols // 2
    rows_two = (groups + 1) * STRIPS
    pitch = sheet.shape[0] // 3
    windows = -(-(half + 2) // LANES)
    turns = (rows // 2 + 2) // TURN
    strip = groups + 3
    lane = lax.broadcasted_iota(jnp.int32, (8, cols), 1)
    sub = lax.broadcasted_iota(jnp.int32, (8, LANES), 0)
    tile_index = lax.axis_index("tile")
    first_row = tile_index * rows
    total_rows = lax.axis_size("tile") * rows
    first_level = lax.axis_index("group") * levels_here

    def bring(level):
        return [
            pltpu.make_async_copy(ref.at[level], fields.at[f, pl.ds(PAD, rows)], sems.at[f])
            for f, ref in enumerate((east_ref, north_ref, tracer_ref))
        ]

    shore_copy = pltpu.make_async_copy(land_ref, shore, sems.at[3])
    shore_copy.start()
    for copy in bring(0):
        copy.start()

    channels = two_ref.shape[2]
    blank = jnp.zeros((channels, channels), bf16)
    for k in range(16):
        by, bx, py, px = k // 8, k // 4 % 2, k // 2 % 2, k % 2
        for p in range(2):
            row, column = 2 * by + py - p, 2 * bx + px
            pair = [
                two_ref[row, column - par] if 0 <= row < 3 and 0 <= column - par < 3 else blank
                for par in range(2)
            ]
            two[k * channels : (k + 1) * channels, p * LANES : (p + 1) * LANES] = jnp.concatenate(pair, axis=1)
    rough[...] = jnp.zeros_like(rough)
    inputs = one_ref.shape[0]
    none = jnp.zeros((3, channels), f32)
    for c in range(inputs):
        for source in range(4):
            pair = [one_ref[c, source - par] if 0 <= source - par < 3 else none for par in range(2)]
            pair = jnp.concatenate(pair, axis=1)
            for p in range(2):
                start = c * 16 + source * 4 + p
                rough[start : start + 3, p * LANES : (p + 1) * LANES] = pair
    rest = jnp.concatenate([0.5 * low_ref[...]] * 4, axis=1)
    for k in range(3):
        piece = rest.astype(bf16).astype(f32)
        rough[16 * inputs + k : 16 * inputs + k + 1, :] = piece
        rest = rest - piece
    one[...] = rough[...].astype(bf16)
    none = jnp.zeros((4, channels), f32)
    for k in range(32):
        by, bx, par, p, py = k // 16, k // 8 % 2, k // 4 % 2, k // 2 % 2, k % 2
        row = 2 * by + py - p
        pair = [
            three_ref[row, 2 * bx + px - par] if 0 <= row < 3 and 0 <= 2 * bx + px - par < 3 else none
            for px in range(2)
        ]
        start = 32 * by + 16 * bx + 8 * par + 4 * p
        rough[start : start + 4, py * LANES : (py + 1) * LANES] = jnp.concatenate(pair, axis=1)
    three[...] = rough[0:64, :].astype(bf16)
    mid[...] = jnp.concatenate([0.5 * mid_ref[...]] * 4, axis=1)
    comp = lax.broadcasted_iota(jnp.int32, high.shape, 0) & 3
    value = jnp.zeros(high.shape, f32)
    for c in range(high_ref.shape[0]):
        value = jnp.where(comp == c, high_ref[c], value)
    high[...] = value
    w = lax.broadcasted_iota(jnp.int32, (3 * LANES, LANES), 0)
    x = lax.broadcasted_iota(jnp.int32, (3 * LANES, LANES), 1)
    for s in range(4):
        split[:, s * LANES : (s + 1) * LANES] = jnp.where(w == 2 * x - 3 + s + LANES, 1.0, 0.0).astype(bf16)

    at_strip = lax.broadcasted_iota(jnp.int32, (STRIPS, LANES), 0)
    at_lane = lax.broadcasted_iota(jnp.int32, (STRIPS, LANES), 1)
    for tile in range(cols // LANES):
        inside = at_lane + tile * LANES - 2 * groups * at_strip
        for par in range(2):
            for t in range(groups):
                start = par * half + t * STRIPS
                merge[start : start + STRIPS, tile * LANES : (tile + 1) * LANES] = jnp.where(
                    inside == 2 * t + par, 1.0, 0.0
                ).astype(bf16)
    columns = lax.broadcasted_iota(jnp.int32, turned.shape, 2)
    turned[...] = jnp.where((columns >= 48) & (columns < 51), 1.0, 0.0)
    for s in range(4):
        for m in range(windows):
            parts[s, m, 0:LEAD, :] = jnp.zeros((LEAD, LANES), f32)
            parts[s, m, LEAD + 3 * pitch :, :] = jnp.zeros((parts.shape[2] - LEAD - 3 * pitch, LANES), f32)
    sheet[:, 0:LANES] = jnp.zeros((3 * pitch, LANES), f32)
    sheet[:, LANES + cols :] = jnp.zeros((3 * pitch, sheet.shape[1] - LANES - cols), f32)
    for f in range(3):
        low_pad = f * pitch + rows + 2 * HALO
        sheet[low_pad : (f + 1) * pitch, :] = jnp.zeros((pitch - rows - 2 * HALO, sheet.shape[1]), f32)

    shore_copy.wait()
    depths = jnp.concatenate(
        [
            jnp.full((8, rows), depth_ref[tile_index * across + tile], jnp.int32).astype(f32)
            for tile in range(across)
        ],
        axis=1,
    )
    fields[3, PAD - edge : PAD, :] = upper_ref[3 * levels_here]
    fields[3, PAD + rows : PAD + rows + edge, :] = lower_ref[3 * levels_here]
    for r in range(0, rows, 8):
        fields[3, PAD + r : PAD + r + 8, :] = jnp.where(shore[r : r + 8, :] == 1, depths, 0.0)

    def sideways(value):
        left = jnp.where(lane > 0, pltpu.roll(value, 1, 1), 0.0)
        right = jnp.where(lane < cols - 1, pltpu.roll(value, cols - 1, 1), 0.0)
        return left, right

    def wet(number, at):
        return jnp.where(number < fields[3, at : at + 8, :], 1.0, 0.0)

    def advance(level, number):
        copies = bring(level)
        for f, copy in enumerate(copies):
            if level:
                copy.start()
            fields[f, PAD - edge : PAD, :] = upper_ref[f * levels_here + level]
            fields[f, PAD + rows : PAD + rows + edge, :] = lower_ref[f * levels_here + level]
        for copy in copies:
            copy.wait()
        for start in range(-8, rows + 8, 8):
            at = start + PAD

            def around(slot):
                here = fields[slot, at : at + 8, :]
                return (here, fields[slot, at - 1 : at + 7, :], fields[slot, at + 1 : at + 9, :]) + sideways(here)

            def curvature(a):
                return a[2] + a[1] + a[4] + a[3] - 4.0 * a[0]

            east, north, tracer = around(0), around(1), around(2)
            active = wet(number, at)
            row = first_row + start + lax.broadcasted_iota(jnp.int32, (8, cols), 0)
            coriolis = coriolis_base + coriolis_slope * (row.astype(f32) + 0.5) / total_rows
            grad_east = 0.5 * (tracer[2] - tracer[1])
            grad_north = 0.5 * (tracer[4] - tracer[3])
            rate = time_step * active
            news = (
                east[0] + rate * (coriolis * north[0] - grad_east + viscosity * curvature(east)),
                north[0] + rate * (-coriolis * east[0] - grad_north + viscosity * curvature(north)),
                tracer[0]
                + rate * (-(east[0] * grad_east + north[0] * grad_north) + diffusivity * curvature(tracer)),
            )
            for f, (new, out) in enumerate(zip(news, (out_east, out_north, out_tracer), strict=True)):
                if 0 <= start < rows:
                    out[level, start : start + 8, :] = new
                new = new * active
                first, last = max(start, -HALO), min(start + 8, rows + HALO)
                sheet[f * pitch + first + HALO : f * pitch + last + HALO, LANES : LANES + cols] = new[
                    first - start : last - start
                ]

    def split_columns():
        for m in range(windows):
            source = sheet[:, 2 * m * LANES : (2 * m + 3) * LANES].astype(bf16)
            pieces = jnp.dot(source, split[...], preferred_element_type=f32)
            for s in range(4):
                parts[s, m, LEAD : LEAD + 3 * pitch, :] = pieces[:, s * LANES : (s + 1) * LANES]

    def prepare(slot, base, offset):
        flipped, twin = [], slot % 2
        for m in range(windows):
            at = lambda s, first: parts[s, m, pl.ds(base + first, 8), :]
            stack = jnp.concatenate(
                [
                    jnp.where(
                        sub < 4,
                        at(s, LEAD + c * pitch + offset),
                        at(s + 1, LEAD + c * pitch + offset - 4),
                    )
                    for c in range(3)
                    for s in (0, 2)
                ],
                axis=0,
            )
            flipped.append(stack.T)
        flipped = jnp.concatenate(flipped, axis=0)
        for s in range(STRIPS):
            turned[twin, s * strip : s * strip + groups + 8, 0:48] = flipped[s * groups : (s + 1) * groups + 8]
        for t in range(groups + 2):
            ready[slot, t * STRIPS : (t + 1) * STRIPS, :] = turned[twin, pl.ds(t, STRIPS, strip), :].astype(bf16)

    def layer_one(slot, target):
        value = jnp.dot(ready[slot], one[...], preferred_element_type=f32)
        hidden[target] = gate(value).astype(bf16)

    def layer_two(slot):
        gathered = jnp.concatenate(
            [hidden[slot + by, bx * STRIPS : bx * STRIPS + rows_two, :] for by in range(2) for bx in range(2)],
            axis=1,
        )
        value = jnp.dot(gathered, two[...], preferred_element_type=f32)
        top[slot, 0:rows_two, :] = gate(value + mid[...]).astype(bf16)

    def layer_three(slot, base, offset):
        new = lax.dot_general(
            three[...], top[slot], (((1,), (1,)), ((), ())), preferred_element_type=f32
        )
        old = sums[...]
        wide = old[16:32, STRIPS : STRIPS + half] + new[48:64, STRIPS : STRIPS + half]
        value = old[0:16, 0:half] + new[32:48, 0:half] + wide + high[...]
        stress[pl.ds(base + offset, 8), 0:half] = value[0:8]
        stress[pl.ds(base + offset, 8), half:cols] = value[8:16]
        sums[...] = new

    def finish(level, number):
        merged = jnp.dot(stress[8 * (TURN + 1) :, :].astype(bf16), merge[...], preferred_element_type=f32)
        for tile in range(cols // LANES):
            natural[tile] = merged[:, tile * LANES : (tile + 1) * LANES]

        def field(start, shift, comp):
            at = pl.ds(4 * (start + 1 + shift) + comp, 8, 4)
            value = jnp.concatenate([natural[tile, at, :] for tile in range(cols // LANES)], axis=1)
            return value * wet(number, start + PAD + shift)

        for start in range(0, rows, 8):
            rate = eddy_gain * wet(number, start + PAD)
            east_left, east_right = sideways(field(start, 0, 1))
            north_left, north_right = sideways(field(start, 0, 2))
            push_east = 0.5 * (field(start, 1, 0) - field(start, -1, 0)) + 0.5 * (east_right - east_left)
            push_north = 0.5 * (field(start, 1, 1) - field(start, -1, 1)) + 0.5 * (north_right - north_left)
            out_east[level, start : start + 8, :] += rate * push_east
            out_north[level, start : start + 8, :] += rate * push_north

    for level in range(levels_here):
        number = (first_level + level).astype(f32)
        advance(level, number)
        split_columns()
        for slot in range(TURN + 1):
            prepare(slot % TURN, 0, 2 * slot)
            layer_one(slot % TURN, slot)
        for slot in range(TURN):
            prepare(slot, 0, 2 * (TURN + 1 + slot))

        def turn(k, carry):
            at = pl.multiple_of(8 * TURN * k, 16)
            base = 2 * TURN * k
            for i in range(TURN):
                layer_three(i, at, 8 * i)
                layer_two(i)
                if i:
                    layer_one(i - 1, i)
                    prepare(i - 1, base, 2 * (2 * TURN + i))
            hidden[0] = hidden[TURN]
            layer_one(TURN - 1, TURN)
            prepare(TURN - 1, base, 6 * TURN)
            return carry

        lax.fori_loop(0, turns, turn, 0)
        for i in range(TURN):
            layer_three(i, 8 * TURN * turns, 8 * i)
        finish(level, number)


def ocean_step(tile_depth, fields, land, upper, lower, weights):
    conv_one, bias_one, conv_two, bias_two, conv_three, bias_three = weights
    levels_here, rows, cols = fields[0].shape
    hidden = conv_two.shape[0]
    width = 4 * hidden
    half = cols // 2
    groups = half // STRIPS
    windows = -(-(half + 2) // LANES)
    turns = (rows // 2 + 2) // TURN
    pitch = rows + 4 * HALO
    f32, bf16 = jnp.float32, jnp.bfloat16
    one = conv_one.transpose(1, 3, 2, 0).astype(f32) * 0.5
    two = conv_two.transpose(2, 3, 1, 0) * jnp.asarray(0.5, bf16)
    three = jnp.pad(conv_three.transpose(2, 3, 0, 1).astype(f32), ((0, 0), (0, 0), (0, 4 - conv_three.shape[0]), (0, 0)))
    vmem = pl.BlockSpec(memory_space=pltpu.VMEM)
    smem = pl.BlockSpec(memory_space=pltpu.SMEM)
    far = pl.BlockSpec(memory_space=pltpu.HBM)
    field = jax.ShapeDtypeStruct(fields[0].shape, f32)
    top_rows = (groups + 1) * STRIPS
    stress_rows = 8 * TURN * (turns + 1)
    return pl.pallas_call(
        step_kernel,
        out_shape=(field,) * 3,
        in_specs=[smem, smem] + [far] * 4 + [vmem] * 7,
        out_specs=(vmem,) * 3,
        scratch_shapes=[
            pltpu.VMEM((4, rows + 2 * PAD, cols), f32),
            pltpu.VMEM((rows, cols), jnp.int32),
            pltpu.VMEM((cols, cols), bf16),
            pltpu.VMEM((3 * LANES, 4 * LANES), bf16),
            pltpu.VMEM((LANES, width), bf16),
            pltpu.VMEM((64, width), bf16),
            pltpu.VMEM((LANES, width), f32),
            pltpu.VMEM((16, half), f32),
            pltpu.VMEM((1, width), f32),
            pltpu.VMEM((3 * pitch, (2 * windows + 1) * LANES), f32),
            pltpu.VMEM((4, windows, LEAD + 3 * pitch + 8 * TURN, LANES), f32),
            pltpu.VMEM((2, STRIPS * (groups + 3) + 8, LANES), f32),
            pltpu.VMEM((TURN, (groups + 2) * STRIPS, LANES), bf16),
            pltpu.VMEM((4 * width, width), bf16),
            pltpu.VMEM((TURN + 1, (groups + 2) * STRIPS, width), bf16),
            pltpu.VMEM((TURN, top_rows, width), bf16),
            pltpu.VMEM((64, top_rows), f32),
            pltpu.VMEM((stress_rows, cols), f32),
            pltpu.VMEM((cols // LANES, stress_rows - 8 * (TURN + 1), LANES), f32),
            pltpu.SemaphoreType.DMA((4,)),
        ],
        compiler_params=pltpu.CompilerParams(vmem_limit_bytes=44 * 1024 * 1024),
        name="step",
    )(
        tile_depth,
        bias_three,
        *fields,
        land,
        upper,
        lower,
        one,
        bias_one[None],
        two,
        bias_two[None],
        three,
    )


def body(
    velocity_u,
    velocity_v,
    tracer,
    land,
    tile_depth,
    conv_one,
    bias_one,
    conv_two,
    bias_two,
    conv_three,
    bias_three,
):
    fields = (velocity_u, velocity_v, tracer)
    tile_count = lax.axis_size("tile")
    forward = [(i, i + 1) for i in range(tile_count - 1)]
    backward = [(target, source) for source, target in forward]
    first, last = borders(tile_depth, fields, land, EDGE)
    upper = lax.ppermute(last, "tile", forward)
    lower = lax.ppermute(first, "tile", backward)
    weights = (conv_one, bias_one, conv_two, bias_two, conv_three, bias_three)
    return ocean_step(tile_depth, fields, land, upper, lower, weights)


def solution(mesh):
    field = P("group", "tile", None)
    in_specs = (field, field, field, P("tile", None)) + (P(),) * 7
    return jax.shard_map(
        body, mesh=mesh, in_specs=in_specs, out_specs=(field,) * 3, check_vma=False
    )
```

```python
import jax
import jax.numpy as jnp
from jax import lax
from jax.experimental import pallas as pl
from jax.experimental.pallas import tpu as pltpu
from jax.sharding import PartitionSpec as P

time_step = 0.1
viscosity = 0.5
diffusivity = 0.5
eddy_gain = 0.5
coriolis_base = 0.2
coriolis_slope = 0.6

LANES = 128
STRIPS = 16
HALO = 4
PAD = 16
LEAD = 8
EDGE = 8
TURN = 6


def gate(value):
    return value + value * jnp.tanh(value)


def border_kernel(depth_ref, east_ref, north_ref, tracer_ref, land_ref, first_ref, last_ref, shore, sems):
    levels_here, rows, cols = east_ref.shape
    depth = first_ref.shape[1]
    across = cols // rows
    tile_index = lax.axis_index("tile")
    copies = []
    for side, (target, start) in enumerate(((first_ref, 0), (last_ref, rows - depth))):
        at = pl.ds(start, depth)
        for f, ref in enumerate((east_ref, north_ref, tracer_ref)):
            for level in range(levels_here):
                slot = f * levels_here + level
                copies.append(pltpu.make_async_copy(ref.at[level, at], target.at[slot], sems.at[side, slot]))
        copies.append(pltpu.make_async_copy(land_ref.at[at], shore.at[side], sems.at[side, 3 * levels_here]))
    for copy in copies:
        copy.start()
    for copy in copies:
        copy.wait()
    for side, target in enumerate((first_ref, last_ref)):
        for tile in range(across):
            at = slice(tile * rows, (tile + 1) * rows)
            value = jnp.full((depth, rows), depth_ref[tile_index * across + tile], jnp.int32)
            target[3 * levels_here, :, at] = jnp.where(shore[side, :, at] == 1, value, 0).astype(jnp.float32)


def borders(tile_depth, fields, land, depth):
    levels_here, _, cols = fields[0].shape
    count = 3 * levels_here + 1
    edge = jax.ShapeDtypeStruct((count, depth, cols), jnp.float32)
    far = pl.BlockSpec(memory_space=pltpu.HBM)
    vmem = pl.BlockSpec(memory_space=pltpu.VMEM)
    return pl.pallas_call(
        border_kernel,
        out_shape=(edge, edge),
        in_specs=[pl.BlockSpec(memory_space=pltpu.SMEM)] + [far] * 4,
        out_specs=(vmem, vmem),
        scratch_shapes=[pltpu.VMEM((2, depth, cols), jnp.int32), pltpu.SemaphoreType.DMA((2, count))],
        compiler_params=pltpu.CompilerParams(vmem_limit_bytes=62 * 1024 * 1024),
        name="borders",
    )(tile_depth, *fields, land)


def sideways(value, lane):
    cols = value.shape[1]
    left = jnp.where(lane > 0, pltpu.roll(value, 1, 1), 0.0)
    right = jnp.where(lane < cols - 1, pltpu.roll(value, cols - 1, 1), 0.0)
    return left, right


def evolve(fields, at, active, row, rows):
    cols = fields.shape[-1]
    f32 = jnp.float32
    lane = lax.broadcasted_iota(jnp.int32, (8, cols), 1)
    places = (row + lax.broadcasted_iota(jnp.int32, (8, LANES), 0)).astype(f32)
    total_rows = lax.axis_size("tile") * rows
    coriolis = coriolis_base + coriolis_slope * (places + 0.5) / total_rows
    coriolis = jnp.concatenate([coriolis] * (cols // LANES), axis=1)

    def around(f):
        here = fields[f, at : at + 8, :]
        return (here, fields[f, at - 1 : at + 7, :], fields[f, at + 1 : at + 9, :]) + sideways(here, lane)

    def curvature(a):
        return a[2] + a[1] + a[4] + a[3] - 4.0 * a[0]

    east, north, tracer = around(0), around(1), around(2)
    grad_east = 0.5 * (tracer[2] - tracer[1])
    grad_north = 0.5 * (tracer[4] - tracer[3])
    rate = time_step * active
    return (
        east[0] + rate * (coriolis * north[0] - grad_east + viscosity * curvature(east)),
        north[0] + rate * (-coriolis * east[0] - grad_north + viscosity * curvature(north)),
        tracer[0] + rate * (-(east[0] * grad_east + north[0] * grad_north) + diffusivity * curvature(tracer)),
    )


def interior_kernel(
    depth_ref,
    high_ref,
    east_ref,
    north_ref,
    tracer_ref,
    land_ref,
    one_ref,
    low_ref,
    two_ref,
    mid_ref,
    three_ref,
    out_east,
    out_north,
    out_tracer,
    reach,
    sheet,
    one,
    two,
    three,
    mid,
    high,
    split,
    merge,
    fields,
    shore,
    rough,
    sems,
):
    levels_here, rows, cols = east_ref.shape
    across = cols // rows
    f32, bf16 = jnp.float32, jnp.bfloat16
    groups = cols // 2 // STRIPS
    half = cols // 2
    pitch = sheet.shape[1] // 3
    tile_index = lax.axis_index("tile")
    first_level = lax.axis_index("group") * levels_here

    def bring(level):
        return [
            pltpu.make_async_copy(ref.at[level], fields.at[f, pl.ds(PAD, rows)], sems.at[f])
            for f, ref in enumerate((east_ref, north_ref, tracer_ref))
        ]

    shore_copy = pltpu.make_async_copy(land_ref, shore, sems.at[3])
    shore_copy.start()
    for copy in bring(0):
        copy.start()

    channels = two_ref.shape[2]
    blank = jnp.zeros((channels, channels), bf16)
    for k in range(16):
        by, bx, py, px = k // 8, k // 4 % 2, k // 2 % 2, k % 2
        for p in range(2):
            row, column = 2 * by + py - p, 2 * bx + px
            pair = [
                two_ref[row, column - par] if 0 <= row < 3 and 0 <= column - par < 3 else blank
                for par in range(2)
            ]
            two[k * channels : (k + 1) * channels, p * LANES : (p + 1) * LANES] = jnp.concatenate(pair, axis=1)
    rough[...] = jnp.zeros_like(rough)
    inputs = one_ref.shape[0]
    none = jnp.zeros((3, channels), f32)
    for c in range(inputs):
        for source in range(4):
            pair = [one_ref[c, source - par] if 0 <= source - par < 3 else none for par in range(2)]
            pair = jnp.concatenate(pair, axis=1)
            for p in range(2):
                start = c * 16 + source * 4 + p
                rough[start : start + 3, p * LANES : (p + 1) * LANES] = pair
    rest = jnp.concatenate([0.5 * low_ref[...]] * 4, axis=1)
    for k in range(3):
        piece = rest.astype(bf16).astype(f32)
        rough[16 * inputs + k : 16 * inputs + k + 1, :] = piece
        rest = rest - piece
    one[...] = rough[...].astype(bf16)
    none = jnp.zeros((4, channels), f32)
    for k in range(32):
        by, bx, par, p, py = k // 16, k // 8 % 2, k // 4 % 2, k // 2 % 2, k % 2
        row = 2 * by + py - p
        pair = [
            three_ref[row, 2 * bx + px - par] if 0 <= row < 3 and 0 <= 2 * bx + px - par < 3 else none
            for px in range(2)
        ]
        start = 32 * by + 16 * bx + 8 * par + 4 * p
        rough[start : start + 4, py * LANES : (py + 1) * LANES] = jnp.concatenate(pair, axis=1)
    three[...] = rough[0:64, :].astype(bf16)
    mid[...] = jnp.concatenate([0.5 * mid_ref[...]] * 4, axis=1)
    comp = lax.broadcasted_iota(jnp.int32, high.shape, 0) & 3
    value = jnp.zeros(high.shape, f32)
    for c in range(high_ref.shape[0]):
        value = jnp.where(comp == c, high_ref[c], value)
    high[...] = value
    w = lax.broadcasted_iota(jnp.int32, (3 * LANES, LANES), 0)
    x = lax.broadcasted_iota(jnp.int32, (3 * LANES, LANES), 1)
    for s in range(4):
        split[:, s * LANES : (s + 1) * LANES] = jnp.where(w == 2 * x - 3 + s + LANES, 1.0, 0.0).astype(bf16)

    at_strip = lax.broadcasted_iota(jnp.int32, (STRIPS, LANES), 0)
    at_lane = lax.broadcasted_iota(jnp.int32, (STRIPS, LANES), 1)
    for tile in range(cols // LANES):
        inside = at_lane + tile * LANES - 2 * groups * at_strip
        for par in range(2):
            for t in range(groups):
                start = par * half + t * STRIPS
                merge[start : start + STRIPS, tile * LANES : (tile + 1) * LANES] = jnp.where(
                    inside == 2 * t + par, 1.0, 0.0
                ).astype(bf16)
    for level in range(levels_here):
        sheet[level, :, 0:LANES] = jnp.zeros((3 * pitch, LANES), f32)
        sheet[level, :, LANES + cols :] = jnp.zeros((3 * pitch, sheet.shape[2] - LANES - cols), f32)
        for f in range(3):
            low_pad = f * pitch + rows + 2 * HALO
            sheet[level, low_pad : (f + 1) * pitch, :] = jnp.zeros((pitch - rows - 2 * HALO, sheet.shape[2]), f32)
            sheet[level, f * pitch : f * pitch + HALO, :] = jnp.zeros((HALO, sheet.shape[2]), f32)
            low_pad = f * pitch + rows + HALO
            sheet[level, low_pad : low_pad + HALO, :] = jnp.zeros((HALO, sheet.shape[2]), f32)
    for f in range(3):
        fields[f, PAD - 8 : PAD, :] = jnp.zeros((8, cols), f32)
        fields[f, PAD + rows : PAD + rows + 8, :] = jnp.zeros((8, cols), f32)

    shore_copy.wait()
    depths = jnp.concatenate(
        [
            jnp.full((8, rows), depth_ref[tile_index * across + tile], jnp.int32).astype(f32)
            for tile in range(across)
        ],
        axis=1,
    )
    for r in range(0, rows, 8):
        reach[r : r + 8, :] = jnp.where(shore[r : r + 8, :] == 1, depths, 0.0)

    for level in range(levels_here):
        copies = bring(level)
        for copy in copies:
            if level:
                copy.start()
        for copy in copies:
            copy.wait()
        number = (first_level + level).astype(f32)
        for start in range(0, rows, 8):
            active = jnp.where(number < reach[start : start + 8, :], 1.0, 0.0)
            news = evolve(fields, start + PAD, active, tile_index * rows + start, rows)
            for f, (new, out) in enumerate(zip(news, (out_east, out_north, out_tracer), strict=True)):
                out[level, start : start + 8, :] = new
                at = f * pitch + start + HALO
                sheet[level, at : at + 8, LANES : LANES + cols] = new * active


def step_kernel(
    east_ref,
    north_ref,
    tracer_ref,
    reach_ref,
    sheet,
    one,
    two,
    three,
    mid,
    high,
    split,
    merge,
    upper_ref,
    first_ref,
    last_ref,
    lower_ref,
    out_east,
    out_north,
    out_tracer,
    edges,
    rim,
    reach,
    parts,
    turned,
    ready,
    hidden,
    top,
    sums,
    stress,
    natural,
):
    levels_here, rows, cols = east_ref.shape
    depth = upper_ref.shape[1]
    f32, bf16 = jnp.float32, jnp.bfloat16
    groups = cols // 2 // STRIPS
    half = cols // 2
    rows_two = (groups + 1) * STRIPS
    pitch = sheet.shape[1] // 3
    windows = -(-(half + 2) // LANES)
    turns = (rows // 2 + 2) // TURN
    strip = groups + 3
    lane = lax.broadcasted_iota(jnp.int32, (8, cols), 1)
    sub = lax.broadcasted_iota(jnp.int32, (8, LANES), 0)
    line = lax.broadcasted_iota(jnp.int32, (8, cols), 0)
    first_row = lax.axis_index("tile") * rows
    first_level = lax.axis_index("group") * levels_here

    columns = lax.broadcasted_iota(jnp.int32, turned.shape, 2)
    turned[...] = jnp.where((columns >= 48) & (columns < 51), 1.0, 0.0)
    for s in range(4):
        for m in range(windows):
            parts[s, m, 0:LEAD, :] = jnp.zeros((LEAD, LANES), f32)
            parts[s, m, LEAD + 3 * pitch :, :] = jnp.zeros((parts.shape[2] - LEAD - 3 * pitch, LANES), f32)
    reach[PAD - 8 : PAD, :] = upper_ref[3 * levels_here]
    reach[PAD + rows : PAD + rows + 8, :] = lower_ref[3 * levels_here]
    for r in range(0, rows, 8):
        reach[PAD + r : PAD + r + 8, :] = reach_ref[r : r + 8, :]

    def wet(number, at):
        return jnp.where(number < reach[at : at + 8, :], 1.0, 0.0)

    def rims(level, number):
        fixed = {}
        zero = jnp.zeros((8, cols), f32)
        rim[:, 0:LANES] = jnp.zeros((rim.shape[0], LANES), f32)
        rim[:, LANES + cols :] = jnp.zeros((rim.shape[0], rim.shape[1] - LANES - cols), f32)
        for side, (outer, inner, start) in enumerate(((upper_ref, first_ref, -8), (last_ref, lower_ref, rows - 8))):
            for f in range(3):
                edges[f, 0:8, :] = zero
                edges[f, 8:16, :] = outer[f * levels_here + level]
                edges[f, 16:24, :] = inner[f * levels_here + level]
                edges[f, 24:32, :] = zero
            active = [wet(number, start + PAD + r) for r in (0, 8)]
            news = [evolve(edges, 8 + r, active[r // 8], first_row + start + r, rows) for r in (0, 8)]
            for f, ref in enumerate((east_ref, north_ref, tracer_ref)):
                if side == 0:
                    kept = jnp.where(line == 0, news[1][f], ref[level, 0:8, :])
                    features = jnp.concatenate([(news[0][f] * active[0])[8 - HALO :], (kept * active[1])[:HALO]])
                else:
                    kept = jnp.where(line == 7, news[0][f], ref[level, rows - 8 : rows, :])
                    features = jnp.concatenate([(kept * active[0])[8 - HALO :], (news[1][f] * active[1])[:HALO]])
                fixed[f, side] = kept
                at = (3 * side + f) * 8
                rim[at : at + 8, LANES : LANES + cols] = features
        for f, out in enumerate((out_east, out_north, out_tracer)):
            out[level, 0:8, :] = fixed[f, 0]
            out[level, rows - 8 : rows, :] = fixed[f, 1]
        for start in range(8, rows - 8, 8):
            out_tracer[level, start : start + 8, :] = tracer_ref[level, start : start + 8, :]

    def split_columns(level):
        for m in range(windows):
            at = slice(2 * m * LANES, (2 * m + 3) * LANES)
            pieces = jnp.dot(sheet[level, :, at].astype(bf16), split[...], preferred_element_type=f32)
            for s in range(4):
                parts[s, m, LEAD : LEAD + 3 * pitch, :] = pieces[:, s * LANES : (s + 1) * LANES]
        for m in range(windows):
            at = slice(2 * m * LANES, (2 * m + 3) * LANES)
            pieces = jnp.dot(rim[:, at].astype(bf16), split[...], preferred_element_type=f32)
            for s in range(4):
                for side in range(2):
                    for f in range(3):
                        start, from_ = LEAD + f * pitch + side * rows, (3 * side + f) * 8
                        parts[s, m, start : start + 8, :] = pieces[from_ : from_ + 8, s * LANES : (s + 1) * LANES]

    def prepare(slot, base, offset):
        flipped, twin = [], slot % 2
        for m in range(windows):
            at = lambda s, first: parts[s, m, pl.ds(base + first, 8), :]
            stack = jnp.concatenate(
                [
                    jnp.where(
                        sub < 4,
                        at(s, LEAD + c * pitch + offset),
                        at(s + 1, LEAD + c * pitch + offset - 4),
                    )
                    for c in range(3)
                    for s in (0, 2)
                ],
                axis=0,
            )
            flipped.append(stack.T)
        flipped = jnp.concatenate(flipped, axis=0)
        for s in range(STRIPS):
            turned[twin, s * strip : s * strip + groups + 8, 0:48] = flipped[s * groups : (s + 1) * groups + 8]
        for t in range(groups + 2):
            ready[slot, t * STRIPS : (t + 1) * STRIPS, :] = turned[twin, pl.ds(t, STRIPS, strip), :].astype(bf16)

    def layer_one(slot, target):
        value = jnp.dot(ready[slot], one[...], preferred_element_type=f32)
        hidden[target] = gate(value).astype(bf16)

    def layer_two(slot):
        gathered = jnp.concatenate(
            [hidden[slot + by, bx * STRIPS : bx * STRIPS + rows_two, :] for by in range(2) for bx in range(2)],
            axis=1,
        )
        value = jnp.dot(gathered, two[...], preferred_element_type=f32)
        top[slot, 0:rows_two, :] = gate(value + mid[...]).astype(bf16)

    def layer_three(slot, base, offset):
        new = lax.dot_general(
            three[...], top[slot], (((1,), (1,)), ((), ())), preferred_element_type=f32
        )
        old = sums[...]
        wide = old[16:32, STRIPS : STRIPS + half] + new[48:64, STRIPS : STRIPS + half]
        value = old[0:16, 0:half] + new[32:48, 0:half] + wide + high[...]
        stress[pl.ds(base + offset, 8), 0:half] = value[0:8]
        stress[pl.ds(base + offset, 8), half:cols] = value[8:16]
        sums[...] = new

    def finish(level, number):
        merged = jnp.dot(stress[8 * (TURN + 1) :, :].astype(bf16), merge[...], preferred_element_type=f32)
        for tile in range(cols // LANES):
            natural[tile] = merged[:, tile * LANES : (tile + 1) * LANES]

        def field(start, shift, comp):
            at = pl.ds(4 * (start + 1 + shift) + comp, 8, 4)
            value = jnp.concatenate([natural[tile, at, :] for tile in range(cols // LANES)], axis=1)
            return value * wet(number, start + PAD + shift)

        for start in range(0, rows, 8):
            rate = eddy_gain * wet(number, start + PAD)
            east_left, east_right = sideways(field(start, 0, 1), lane)
            north_left, north_right = sideways(field(start, 0, 2), lane)
            push_east = 0.5 * (field(start, 1, 0) - field(start, -1, 0)) + 0.5 * (east_right - east_left)
            push_north = 0.5 * (field(start, 1, 1) - field(start, -1, 1)) + 0.5 * (north_right - north_left)
            inside = 0 < start < rows - 8
            for out, ref, push in ((out_east, east_ref, push_east), (out_north, north_ref, push_north)):
                base = (ref if inside else out)[level, start : start + 8, :]
                out[level, start : start + 8, :] = base + rate * push

    for level in range(levels_here):
        number = (first_level + level).astype(f32)
        rims(level, number)
        split_columns(level)
        for slot in range(TURN + 1):
            prepare(slot % TURN, 0, 2 * slot)
            layer_one(slot % TURN, slot)
        for slot in range(TURN):
            prepare(slot, 0, 2 * (TURN + 1 + slot))

        def turn(k, carry):
            at = pl.multiple_of(8 * TURN * k, 16)
            base = 2 * TURN * k
            for i in range(TURN):
                layer_three(i, at, 8 * i)
                layer_two(i)
                if i:
                    layer_one(i - 1, i)
                    prepare(i - 1, base, 2 * (2 * TURN + i))
            hidden[0] = hidden[TURN]
            layer_one(TURN - 1, TURN)
            prepare(TURN - 1, base, 6 * TURN)
            return carry

        lax.fori_loop(0, turns, turn, 0)
        for i in range(TURN):
            layer_three(i, 8 * TURN * turns, 8 * i)
        finish(level, number)


def ocean_step(tile_depth, fields, land, upper, first, last, lower, weights):
    conv_one, bias_one, conv_two, bias_two, conv_three, bias_three = weights
    levels_here, rows, cols = fields[0].shape
    hidden = conv_two.shape[0]
    width = 4 * hidden
    half = cols // 2
    groups = half // STRIPS
    windows = -(-(half + 2) // LANES)
    turns = (rows // 2 + 2) // TURN
    pitch = rows + 4 * HALO
    f32, bf16 = jnp.float32, jnp.bfloat16
    one = conv_one.transpose(1, 3, 2, 0).astype(f32) * 0.5
    two = conv_two.transpose(2, 3, 1, 0) * jnp.asarray(0.5, bf16)
    three = jnp.pad(conv_three.transpose(2, 3, 0, 1).astype(f32), ((0, 0), (0, 0), (0, 4 - conv_three.shape[0]), (0, 0)))
    vmem = pl.BlockSpec(memory_space=pltpu.VMEM)
    smem = pl.BlockSpec(memory_space=pltpu.SMEM)
    far = pl.BlockSpec(memory_space=pltpu.HBM)
    shape = jax.ShapeDtypeStruct
    field = shape(fields[0].shape, f32)
    top_rows = (groups + 1) * STRIPS
    stress_rows = 8 * TURN * (turns + 1)
    inside = pl.pallas_call(
        interior_kernel,
        out_shape=(
            field,
            field,
            field,
            shape((rows, cols), f32),
            shape((levels_here, 3 * pitch, (2 * windows + 1) * LANES), f32),
            shape((LANES, width), bf16),
            shape((4 * width, width), bf16),
            shape((64, width), bf16),
            shape((1, width), f32),
            shape((16, half), f32),
            shape((3 * LANES, 4 * LANES), bf16),
            shape((cols, cols), bf16),
        ),
        in_specs=[smem, smem] + [far] * 4 + [vmem] * 5,
        out_specs=(vmem,) * 12,
        scratch_shapes=[
            pltpu.VMEM((3, rows + 2 * PAD, cols), f32),
            pltpu.VMEM((rows, cols), jnp.int32),
            pltpu.VMEM((LANES, width), f32),
            pltpu.SemaphoreType.DMA((4,)),
        ],
        cost_estimate=pl.CostEstimate(flops=20_000_000, bytes_accessed=12_000_000, transcendentals=0),
        compiler_params=pltpu.CompilerParams(vmem_limit_bytes=16 * 1024 * 1024),
        name="inside",
    )(tile_depth, bias_three, *fields, land, one, bias_one[None], two, bias_two[None], three)
    return pl.pallas_call(
        step_kernel,
        out_shape=(field,) * 3,
        in_specs=[vmem] * 16,
        out_specs=(vmem,) * 3,
        scratch_shapes=[
            pltpu.VMEM((3, 32, cols), f32),
            pltpu.VMEM((48, (2 * windows + 1) * LANES), f32),
            pltpu.VMEM((rows + 2 * PAD, cols), f32),
            pltpu.VMEM((4, windows, LEAD + 3 * pitch + 8 * TURN, LANES), f32),
            pltpu.VMEM((2, STRIPS * (groups + 3) + 8, LANES), f32),
            pltpu.VMEM((TURN, (groups + 2) * STRIPS, LANES), bf16),
            pltpu.VMEM((TURN + 1, (groups + 2) * STRIPS, width), bf16),
            pltpu.VMEM((TURN, top_rows, width), bf16),
            pltpu.VMEM((64, top_rows), f32),
            pltpu.VMEM((stress_rows, cols), f32),
            pltpu.VMEM((cols // LANES, stress_rows - 8 * (TURN + 1), LANES), f32),
        ],
        compiler_params=pltpu.CompilerParams(vmem_limit_bytes=40 * 1024 * 1024),
        name="step",
    )(*inside, upper, first, last, lower)


def body(
    velocity_u,
    velocity_v,
    tracer,
    land,
    tile_depth,
    conv_one,
    bias_one,
    conv_two,
    bias_two,
    conv_three,
    bias_three,
):
    fields = (velocity_u, velocity_v, tracer)
    tile_count = lax.axis_size("tile")
    forward = [(i, i + 1) for i in range(tile_count - 1)]
    backward = [(target, source) for source, target in forward]
    first, last = borders(tile_depth, fields, land, EDGE)
    upper = lax.ppermute(last, "tile", forward)
    lower = lax.ppermute(first, "tile", backward)
    weights = (conv_one, bias_one, conv_two, bias_two, conv_three, bias_three)
    return ocean_step(tile_depth, fields, land, upper, first, last, lower, weights)


def solution(mesh):
    field = P("group", "tile", None)
    in_specs = (field, field, field, P("tile", None)) + (P(),) * 7
    return jax.shard_map(
        body, mesh=mesh, in_specs=in_specs, out_specs=(field,) * 3, check_vma=False
    )
```

```python
import jax
import jax.numpy as jnp
from jax import lax
from jax.experimental import pallas as pl
from jax.experimental.pallas import tpu as pltpu
from jax.sharding import PartitionSpec as P

time_step = 0.1
viscosity = 0.5
diffusivity = 0.5
eddy_gain = 0.5
coriolis_base = 0.2
coriolis_slope = 0.6

LANES = 128
STRIPS = 16
HALO = 4
PAD = 16
LEAD = 8
EDGE = 8
TURN = 6


def gate(value):
    return value + value * jnp.tanh(value)


def border_kernel(depth_ref, east_ref, north_ref, tracer_ref, land_ref, first_ref, last_ref, shore, sems):
    levels_here, rows, cols = east_ref.shape
    depth = first_ref.shape[1]
    across = cols // rows
    tile_index = lax.axis_index("tile")
    copies = []
    for side, (target, start) in enumerate(((first_ref, 0), (last_ref, rows - depth))):
        at = pl.ds(start, depth)
        for f, ref in enumerate((east_ref, north_ref, tracer_ref)):
            for level in range(levels_here):
                slot = f * levels_here + level
                copies.append(pltpu.make_async_copy(ref.at[level, at], target.at[slot], sems.at[side, slot]))
        copies.append(pltpu.make_async_copy(land_ref.at[at], shore.at[side], sems.at[side, 3 * levels_here]))
    for copy in copies:
        copy.start()
    for copy in copies:
        copy.wait()
    for side, target in enumerate((first_ref, last_ref)):
        for tile in range(across):
            at = slice(tile * rows, (tile + 1) * rows)
            value = jnp.full((depth, rows), depth_ref[tile_index * across + tile], jnp.int32)
            target[3 * levels_here, :, at] = jnp.where(shore[side, :, at] == 1, value, 0).astype(jnp.float32)


def borders(tile_depth, fields, land, depth):
    levels_here, _, cols = fields[0].shape
    count = 3 * levels_here + 1
    edge = jax.ShapeDtypeStruct((count, depth, cols), jnp.float32)
    far = pl.BlockSpec(memory_space=pltpu.HBM)
    vmem = pl.BlockSpec(memory_space=pltpu.VMEM)
    return pl.pallas_call(
        border_kernel,
        out_shape=(edge, edge),
        in_specs=[pl.BlockSpec(memory_space=pltpu.SMEM)] + [far] * 4,
        out_specs=(vmem, vmem),
        scratch_shapes=[pltpu.VMEM((2, depth, cols), jnp.int32), pltpu.SemaphoreType.DMA((2, count))],
        compiler_params=pltpu.CompilerParams(vmem_limit_bytes=62 * 1024 * 1024),
        name="borders",
    )(tile_depth, *(pltpu.with_memory_space_constraint(array, pltpu.HBM) for array in (*fields, land)))


def sideways(value, lane):
    cols = value.shape[1]
    left = jnp.where(lane > 0, pltpu.roll(value, 1, 1), 0.0)
    right = jnp.where(lane < cols - 1, pltpu.roll(value, cols - 1, 1), 0.0)
    return left, right


def evolve(fields, at, active, row, rows):
    cols = fields.shape[-1]
    f32 = jnp.float32
    lane = lax.broadcasted_iota(jnp.int32, (8, cols), 1)
    places = (row + lax.broadcasted_iota(jnp.int32, (8, LANES), 0)).astype(f32)
    total_rows = lax.axis_size("tile") * rows
    coriolis = coriolis_base + coriolis_slope * (places + 0.5) / total_rows
    coriolis = jnp.concatenate([coriolis] * (cols // LANES), axis=1)

    def around(f):
        here = fields[f, at : at + 8, :]
        return (here, fields[f, at - 1 : at + 7, :], fields[f, at + 1 : at + 9, :]) + sideways(here, lane)

    def curvature(a):
        return a[2] + a[1] + a[4] + a[3] - 4.0 * a[0]

    east, north, tracer = around(0), around(1), around(2)
    grad_east = 0.5 * (tracer[2] - tracer[1])
    grad_north = 0.5 * (tracer[4] - tracer[3])
    rate = time_step * active
    return (
        east[0] + rate * (coriolis * north[0] - grad_east + viscosity * curvature(east)),
        north[0] + rate * (-coriolis * east[0] - grad_north + viscosity * curvature(north)),
        tracer[0] + rate * (-(east[0] * grad_east + north[0] * grad_north) + diffusivity * curvature(tracer)),
    )


def interior_kernel(
    depth_ref,
    high_ref,
    east_ref,
    north_ref,
    tracer_ref,
    land_ref,
    two_ref,
    one_ref,
    low_ref,
    mid_ref,
    three_ref,
    out_east,
    out_north,
    out_tracer,
    reach,
    sheet,
    one,
    two,
    three,
    mid,
    high,
    split,
    merge,
    ends,
    fields,
    shore,
    rough,
    taps,
    sems,
):
    levels_here, rows, cols = east_ref.shape
    across = cols // rows
    f32, bf16 = jnp.float32, jnp.bfloat16
    groups = cols // 2 // STRIPS
    half = cols // 2
    pitch = sheet.shape[1] // 3
    tile_index = lax.axis_index("tile")
    first_level = lax.axis_index("group") * levels_here

    def bring(level):
        return [
            pltpu.make_async_copy(ref.at[level], fields.at[f, pl.ds(PAD, rows)], sems.at[f])
            for f, ref in enumerate((east_ref, north_ref, tracer_ref))
        ]

    taps_copy = pltpu.make_async_copy(two_ref, taps, sems.at[4])
    shore_copy = pltpu.make_async_copy(land_ref, shore, sems.at[3])
    taps_copy.start()
    shore_copy.start()
    for copy in bring(0):
        copy.start()

    channels = two_ref.shape[2]
    rough[...] = jnp.zeros_like(rough)
    inputs = one_ref.shape[0]
    kernels = [[one_ref[c, r].astype(f32) * 0.5 for r in range(3)] for c in range(inputs)]
    kernels = [[jnp.concatenate([k[r][x : x + 1] for r in range(3)], axis=0) for x in range(3)] for k in kernels]
    none = jnp.zeros((3, channels), f32)
    for c in range(inputs):
        for source in range(4):
            pair = [kernels[c][source - par] if 0 <= source - par < 3 else none for par in range(2)]
            pair = jnp.concatenate(pair, axis=1)
            for p in range(2):
                start = c * 16 + source * 4 + p
                rough[start : start + 3, p * LANES : (p + 1) * LANES] = pair
    rest = jnp.concatenate([0.5 * low_ref[...]] * 4, axis=1)
    for k in range(3):
        piece = rest.astype(bf16).astype(f32)
        rough[16 * inputs + k : 16 * inputs + k + 1, :] = piece
        rest = rest - piece
    one[...] = rough[...].astype(bf16)
    none = jnp.zeros((4, channels), f32)
    outputs = three_ref.shape[0]
    kernels = [[three_ref[c, r].astype(f32) for r in range(3)] for c in range(outputs)]
    kernels = [
        [
            jnp.concatenate([k[r][x : x + 1] for k in kernels] + [none[outputs:]], axis=0)
            for x in range(3)
        ]
        for r in range(3)
    ]
    for k in range(32):
        by, bx, par, p, py = k // 16, k // 8 % 2, k // 4 % 2, k // 2 % 2, k % 2
        row = 2 * by + py - p
        pair = [
            kernels[row][2 * bx + px - par] if 0 <= row < 3 and 0 <= 2 * bx + px - par < 3 else none
            for px in range(2)
        ]
        start = 32 * by + 16 * bx + 8 * par + 4 * p
        rough[start : start + 4, py * LANES : (py + 1) * LANES] = jnp.concatenate(pair, axis=1)
    three[...] = rough[0:64, :].astype(bf16)
    mid[...] = jnp.concatenate([0.5 * mid_ref[...]] * 4, axis=1)
    comp = lax.broadcasted_iota(jnp.int32, high.shape, 0) & 3
    value = jnp.zeros(high.shape, f32)
    for c in range(high_ref.shape[0]):
        value = jnp.where(comp == c, high_ref[c], value)
    high[...] = value
    w = lax.broadcasted_iota(jnp.int32, (3 * LANES, LANES), 0)
    x = lax.broadcasted_iota(jnp.int32, (3 * LANES, LANES), 1)
    for s in range(4):
        split[:, s * LANES : (s + 1) * LANES] = jnp.where(w == 2 * x - 3 + s + LANES, 1.0, 0.0).astype(bf16)

    taps_copy.wait()
    flat = [[(taps[r, c].astype(f32) * 0.5).T.astype(bf16) for c in range(3)] for r in range(3)]
    blank = jnp.zeros((channels, channels), bf16)
    for k in range(16):
        by, bx, py, px = k // 8, k // 4 % 2, k // 2 % 2, k % 2
        for p in range(2):
            row, column = 2 * by + py - p, 2 * bx + px
            pair = [
                flat[row][column - par] if 0 <= row < 3 and 0 <= column - par < 3 else blank
                for par in range(2)
            ]
            two[k * channels : (k + 1) * channels, p * LANES : (p + 1) * LANES] = jnp.concatenate(pair, axis=1)
    at_strip = lax.broadcasted_iota(jnp.int32, (STRIPS, LANES), 0)
    at_lane = lax.broadcasted_iota(jnp.int32, (STRIPS, LANES), 1)
    for tile in range(cols // LANES):
        inside = at_lane + tile * LANES - 2 * groups * at_strip
        for par in range(2):
            for t in range(groups):
                start = par * half + t * STRIPS
                merge[start : start + STRIPS, tile * LANES : (tile + 1) * LANES] = jnp.where(
                    inside == 2 * t + par, 1.0, 0.0
                ).astype(bf16)
    for level in range(levels_here):
        sheet[level, :, 0:LANES] = jnp.zeros((3 * pitch, LANES), f32)
        sheet[level, :, LANES + cols :] = jnp.zeros((3 * pitch, sheet.shape[2] - LANES - cols), f32)
        for f in range(3):
            low_pad = f * pitch + rows + 2 * HALO
            sheet[level, low_pad : (f + 1) * pitch, :] = jnp.zeros((pitch - rows - 2 * HALO, sheet.shape[2]), f32)
            sheet[level, f * pitch : f * pitch + HALO, :] = jnp.zeros((HALO, sheet.shape[2]), f32)
            low_pad = f * pitch + rows + HALO
            sheet[level, low_pad : low_pad + HALO, :] = jnp.zeros((HALO, sheet.shape[2]), f32)
    for f in range(3):
        fields[f, PAD - 8 : PAD, :] = jnp.zeros((8, cols), f32)
        fields[f, PAD + rows : PAD + rows + 8, :] = jnp.zeros((8, cols), f32)

    shore_copy.wait()
    depths = jnp.concatenate(
        [
            jnp.full((8, rows), depth_ref[tile_index * across + tile], jnp.int32).astype(f32)
            for tile in range(across)
        ],
        axis=1,
    )
    for r in range(0, rows, 8):
        reach[r : r + 8, :] = jnp.where(shore[r : r + 8, :] == 1, depths, 0.0)

    for level in range(levels_here):
        copies = bring(level)
        for copy in copies:
            if level:
                copy.start()
        for copy in copies:
            copy.wait()
        for f in range(3):
            ends[0, f * levels_here + level] = fields[f, PAD : PAD + 8, :]
            ends[1, f * levels_here + level] = fields[f, PAD + rows - 8 : PAD + rows, :]
        number = (first_level + level).astype(f32)
        for start in range(0, rows, 8):
            active = jnp.where(number < reach[start : start + 8, :], 1.0, 0.0)
            news = evolve(fields, start + PAD, active, tile_index * rows + start, rows)
            for f, (new, out) in enumerate(zip(news, (out_east, out_north, out_tracer), strict=True)):
                out[level, start : start + 8, :] = new
                at = f * pitch + start + HALO
                sheet[level, at : at + 8, LANES : LANES + cols] = new * active


def step_kernel(
    east_ref,
    north_ref,
    tracer_ref,
    reach_ref,
    sheet,
    one,
    two,
    three,
    mid,
    high,
    split,
    merge,
    ends,
    upper_ref,
    lower_ref,
    out_east,
    out_north,
    out_tracer,
    edges,
    rim,
    reach,
    parts,
    turned,
    ready,
    hidden,
    top,
    sums,
    stress,
    natural,
):
    levels_here, rows, cols = east_ref.shape
    depth = upper_ref.shape[1]
    f32, bf16 = jnp.float32, jnp.bfloat16
    groups = cols // 2 // STRIPS
    half = cols // 2
    rows_two = (groups + 1) * STRIPS
    pitch = sheet.shape[1] // 3
    windows = -(-(half + 2) // LANES)
    turns = (rows // 2 + 2) // TURN
    strip = groups + 3
    lane = lax.broadcasted_iota(jnp.int32, (8, cols), 1)
    sub = lax.broadcasted_iota(jnp.int32, (8, LANES), 0)
    line = lax.broadcasted_iota(jnp.int32, (8, cols), 0)
    first_row = lax.axis_index("tile") * rows
    first_level = lax.axis_index("group") * levels_here

    columns = lax.broadcasted_iota(jnp.int32, turned.shape, 2)
    turned[...] = jnp.where((columns >= 48) & (columns < 51), 1.0, 0.0)
    for s in range(4):
        for m in range(windows):
            parts[s, m, 0:LEAD, :] = jnp.zeros((LEAD, LANES), f32)
            parts[s, m, LEAD + 3 * pitch :, :] = jnp.zeros((parts.shape[2] - LEAD - 3 * pitch, LANES), f32)
    reach[PAD - 8 : PAD, :] = upper_ref[3 * levels_here]
    reach[PAD + rows : PAD + rows + 8, :] = lower_ref[3 * levels_here]
    for r in range(0, rows, 8):
        reach[PAD + r : PAD + r + 8, :] = reach_ref[r : r + 8, :]

    def wet(number, at):
        return jnp.where(number < reach[at : at + 8, :], 1.0, 0.0)

    def rims(level, number):
        fixed = {}
        zero = jnp.zeros((8, cols), f32)
        rim[:, 0:LANES] = jnp.zeros((rim.shape[0], LANES), f32)
        rim[:, LANES + cols :] = jnp.zeros((rim.shape[0], rim.shape[1] - LANES - cols), f32)
        for side, (outer, inner, start) in enumerate(
            ((upper_ref, ends.at[0], -8), (ends.at[1], lower_ref, rows - 8))
        ):
            for f in range(3):
                edges[f, 0:8, :] = zero
                edges[f, 8:16, :] = outer[f * levels_here + level]
                edges[f, 16:24, :] = inner[f * levels_here + level]
                edges[f, 24:32, :] = zero
            active = [wet(number, start + PAD + r) for r in (0, 8)]
            news = [evolve(edges, 8 + r, active[r // 8], first_row + start + r, rows) for r in (0, 8)]
            for f, ref in enumerate((east_ref, north_ref, tracer_ref)):
                if side == 0:
                    kept = jnp.where(line == 0, news[1][f], ref[level, 0:8, :])
                    features = jnp.concatenate([(news[0][f] * active[0])[8 - HALO :], (kept * active[1])[:HALO]])
                else:
                    kept = jnp.where(line == 7, news[0][f], ref[level, rows - 8 : rows, :])
                    features = jnp.concatenate([(kept * active[0])[8 - HALO :], (news[1][f] * active[1])[:HALO]])
                fixed[f, side] = kept
                at = (3 * side + f) * 8
                rim[at : at + 8, LANES : LANES + cols] = features
        for f, out in enumerate((out_east, out_north, out_tracer)):
            out[level, 0:8, :] = fixed[f, 0]
            out[level, rows - 8 : rows, :] = fixed[f, 1]
        for start in range(8, rows - 8, 8):
            out_tracer[level, start : start + 8, :] = tracer_ref[level, start : start + 8, :]

    def split_columns(level):
        for m in range(windows):
            at = slice(2 * m * LANES, (2 * m + 3) * LANES)
            pieces = jnp.dot(sheet[level, :, at].astype(bf16), split[...], preferred_element_type=f32)
            for s in range(4):
                parts[s, m, LEAD : LEAD + 3 * pitch, :] = pieces[:, s * LANES : (s + 1) * LANES]
        for m in range(windows):
            at = slice(2 * m * LANES, (2 * m + 3) * LANES)
            pieces = jnp.dot(rim[:, at].astype(bf16), split[...], preferred_element_type=f32)
            for s in range(4):
                for side in range(2):
                    for f in range(3):
                        start, from_ = LEAD + f * pitch + side * rows, (3 * side + f) * 8
                        parts[s, m, start : start + 8, :] = pieces[from_ : from_ + 8, s * LANES : (s + 1) * LANES]

    def prepare(slot, base, offset):
        flipped, twin = [], slot % 2
        for m in range(windows):
            at = lambda s, first: parts[s, m, pl.ds(base + first, 8), :]
            stack = jnp.concatenate(
                [
                    jnp.where(
                        sub < 4,
                        at(s, LEAD + c * pitch + offset),
                        at(s + 1, LEAD + c * pitch + offset - 4),
                    )
                    for c in range(3)
                    for s in (0, 2)
                ],
                axis=0,
            )
            flipped.append(stack.T)
        flipped = jnp.concatenate(flipped, axis=0)
        for s in range(STRIPS):
            turned[twin, s * strip : s * strip + groups + 8, 0:48] = flipped[s * groups : (s + 1) * groups + 8]
        for t in range(groups + 2):
            ready[slot, t * STRIPS : (t + 1) * STRIPS, :] = turned[twin, pl.ds(t, STRIPS, strip), :].astype(bf16)

    def layer_one(slot, target):
        value = jnp.dot(ready[slot], one[...], preferred_element_type=f32)
        hidden[target] = gate(value).astype(bf16)

    def layer_two(slot):
        gathered = jnp.concatenate(
            [hidden[slot + by, bx * STRIPS : bx * STRIPS + rows_two, :] for by in range(2) for bx in range(2)],
            axis=1,
        )
        value = jnp.dot(gathered, two[...], preferred_element_type=f32)
        top[slot, 0:rows_two, :] = gate(value + mid[...]).astype(bf16)

    def tails():
        rows = jnp.concatenate([top[slot, half:rows_two, :] for slot in range(TURN)], axis=0)
        return lax.dot_general(three[...], rows, (((1,), (1,)), ((), ())), preferred_element_type=f32)

    def layer_three(slot, base, offset, tail):
        new = lax.dot_general(
            three[...], top[slot, 0:half, :], (((1,), (1,)), ((), ())), preferred_element_type=f32
        )
        new = jnp.concatenate([new, tail[:, slot * STRIPS : (slot + 1) * STRIPS]], axis=1)
        old = sums[...]
        wide = old[16:32, STRIPS : STRIPS + half] + new[48:64, STRIPS : STRIPS + half]
        value = old[0:16, 0:half] + new[32:48, 0:half] + wide + high[...]
        stress[pl.ds(base + offset, 8), 0:half] = value[0:8]
        stress[pl.ds(base + offset, 8), half:cols] = value[8:16]
        sums[...] = new

    def finish(level, number):
        merged = jnp.dot(stress[8 * (TURN + 1) :, :].astype(bf16), merge[...], preferred_element_type=f32)
        for tile in range(cols // LANES):
            natural[tile] = merged[:, tile * LANES : (tile + 1) * LANES]

        def field(start, shift, comp):
            at = pl.ds(4 * (start + 1 + shift) + comp, 8, 4)
            value = jnp.concatenate([natural[tile, at, :] for tile in range(cols // LANES)], axis=1)
            return value * wet(number, start + PAD + shift)

        for start in range(0, rows, 8):
            rate = eddy_gain * wet(number, start + PAD)
            east_left, east_right = sideways(field(start, 0, 1), lane)
            north_left, north_right = sideways(field(start, 0, 2), lane)
            push_east = 0.5 * (field(start, 1, 0) - field(start, -1, 0)) + 0.5 * (east_right - east_left)
            push_north = 0.5 * (field(start, 1, 1) - field(start, -1, 1)) + 0.5 * (north_right - north_left)
            inside = 0 < start < rows - 8
            for out, ref, push in ((out_east, east_ref, push_east), (out_north, north_ref, push_north)):
                base = (ref if inside else out)[level, start : start + 8, :]
                out[level, start : start + 8, :] = base + rate * push

    for level in range(levels_here):
        number = (first_level + level).astype(f32)
        rims(level, number)
        split_columns(level)
        for slot in range(TURN + 1):
            prepare(slot % TURN, 0, 2 * slot)
            layer_one(slot % TURN, slot)
        for slot in range(TURN):
            prepare(slot, 0, 2 * (TURN + 1 + slot))

        def turn(k, carry):
            at = pl.multiple_of(8 * TURN * k, 16)
            base = 2 * TURN * k
            tail = tails()
            for i in range(TURN):
                layer_three(i, at, 8 * i, tail)
                layer_two(i)
                if i:
                    layer_one(i - 1, i)
                    prepare(i - 1, base, 2 * (2 * TURN + i))
            hidden[0] = hidden[TURN]
            layer_one(TURN - 1, TURN)
            prepare(TURN - 1, base, 6 * TURN)
            return carry

        lax.fori_loop(0, turns, turn, 0)
        tail = tails()
        for i in range(TURN):
            layer_three(i, 8 * TURN * turns, 8 * i, tail)
        finish(level, number)


def ocean_step(tile_depth, fields, land, upper, lower, weights):
    conv_one, bias_one, conv_two, bias_two, conv_three, bias_three = weights
    levels_here, rows, cols = fields[0].shape
    hidden = conv_two.shape[0]
    width = 4 * hidden
    half = cols // 2
    groups = half // STRIPS
    windows = -(-(half + 2) // LANES)
    turns = (rows // 2 + 2) // TURN
    pitch = rows + 4 * HALO
    f32, bf16 = jnp.float32, jnp.bfloat16
    one = conv_one.transpose(1, 2, 3, 0)
    two = conv_two.transpose(2, 3, 0, 1)
    three = conv_three.transpose(0, 2, 3, 1)
    vmem = pl.BlockSpec(memory_space=pltpu.VMEM)
    smem = pl.BlockSpec(memory_space=pltpu.SMEM)
    far = pl.BlockSpec(memory_space=pltpu.HBM)
    shape = jax.ShapeDtypeStruct
    field = shape(fields[0].shape, f32)
    top_rows = (groups + 1) * STRIPS
    stress_rows = 8 * TURN * (turns + 1)
    inside = pl.pallas_call(
        interior_kernel,
        out_shape=(
            field,
            field,
            field,
            shape((rows, cols), f32),
            shape((levels_here, 3 * pitch, (2 * windows + 1) * LANES), f32),
            shape((LANES, width), bf16),
            shape((4 * width, width), bf16),
            shape((64, width), bf16),
            shape((1, width), f32),
            shape((16, half), f32),
            shape((3 * LANES, 4 * LANES), bf16),
            shape((cols, cols), bf16),
            shape((2, 3 * levels_here, 8, cols), f32),
        ),
        in_specs=[smem, smem] + [far] * 5 + [vmem] * 4,
        out_specs=(vmem,) * 13,
        scratch_shapes=[
            pltpu.VMEM((3, rows + 2 * PAD, cols), f32),
            pltpu.VMEM((rows, cols), jnp.int32),
            pltpu.VMEM((LANES, width), f32),
            pltpu.VMEM(two.shape, bf16),
            pltpu.SemaphoreType.DMA((5,)),
        ],
        cost_estimate=pl.CostEstimate(flops=20_000_000, bytes_accessed=12_000_000, transcendentals=0),
        compiler_params=pltpu.CompilerParams(vmem_limit_bytes=16 * 1024 * 1024),
        name="inside",
    )(
        *(
            pltpu.with_memory_space_constraint(array, pltpu.HBM)
            for array in (tile_depth, bias_three, *fields, land, two, one, bias_one[None], bias_two[None], three)
        )
    )
    return pl.pallas_call(
        step_kernel,
        out_shape=(field,) * 3,
        in_specs=[vmem] * 15,
        out_specs=(vmem,) * 3,
        scratch_shapes=[
            pltpu.VMEM((3, 32, cols), f32),
            pltpu.VMEM((48, (2 * windows + 1) * LANES), f32),
            pltpu.VMEM((rows + 2 * PAD, cols), f32),
            pltpu.VMEM((4, windows, LEAD + 3 * pitch + 8 * TURN, LANES), f32),
            pltpu.VMEM((2, STRIPS * (groups + 3) + 8, LANES), f32),
            pltpu.VMEM((TURN, (groups + 2) * STRIPS, LANES), bf16),
            pltpu.VMEM((TURN + 1, (groups + 2) * STRIPS, width), bf16),
            pltpu.VMEM((TURN, top_rows, width), bf16),
            pltpu.VMEM((64, top_rows), f32),
            pltpu.VMEM((stress_rows, cols), f32),
            pltpu.VMEM((cols // LANES, stress_rows - 8 * (TURN + 1), LANES), f32),
        ],
        compiler_params=pltpu.CompilerParams(vmem_limit_bytes=40 * 1024 * 1024),
        name="step",
    )(*inside, upper, lower)


def body(
    velocity_u,
    velocity_v,
    tracer,
    land,
    tile_depth,
    conv_one,
    bias_one,
    conv_two,
    bias_two,
    conv_three,
    bias_three,
):
    fields = (velocity_u, velocity_v, tracer)
    tile_count = lax.axis_size("tile")
    forward = [(i, i + 1) for i in range(tile_count - 1)]
    backward = [(target, source) for source, target in forward]
    first, last = borders(tile_depth, fields, land, EDGE)
    upper = lax.ppermute(last, "tile", forward)
    lower = lax.ppermute(first, "tile", backward)
    weights = (conv_one, bias_one, conv_two, bias_two, conv_three, bias_three)
    return ocean_step(tile_depth, fields, land, upper, lower, weights)


def solution(mesh):
    field = P("group", "tile", None)
    in_specs = (field, field, field, P("tile", None)) + (P(),) * 7
    return jax.shard_map(
        body, mesh=mesh, in_specs=in_specs, out_specs=(field,) * 3, check_vma=False
    )
```

```python
import jax
import jax.numpy as jnp
from jax import lax
from jax.experimental import pallas as pl
from jax.experimental.pallas import tpu as pltpu
from jax.sharding import PartitionSpec as P

time_step = 0.1
viscosity = 0.5
diffusivity = 0.5
eddy_gain = 0.5
coriolis_base = 0.2
coriolis_slope = 0.6

LANES = 128
STRIPS = 16
HALO = 4
PAD = 16
LEAD = 8
EDGE = 8
TURN = 6


def gate(value):
    return value + value * jnp.tanh(value)


def border_kernel(depth_ref, east_ref, north_ref, tracer_ref, land_ref, first_ref, last_ref, shore, sems):
    levels_here, rows, cols = east_ref.shape
    depth = first_ref.shape[1]
    across = cols // rows
    tile_index = lax.axis_index("tile")
    copies = []
    for side, (target, start) in enumerate(((first_ref, 0), (last_ref, rows - depth))):
        at = pl.ds(start, depth)
        for f, ref in enumerate((east_ref, north_ref, tracer_ref)):
            for level in range(levels_here):
                slot = f * levels_here + level
                copies.append(pltpu.make_async_copy(ref.at[level, at], target.at[slot], sems.at[side, slot]))
        copies.append(pltpu.make_async_copy(land_ref.at[at], shore.at[side], sems.at[side, 3 * levels_here]))
    for copy in copies:
        copy.start()
    for copy in copies:
        copy.wait()
    for side, target in enumerate((first_ref, last_ref)):
        for tile in range(across):
            at = slice(tile * rows, (tile + 1) * rows)
            value = jnp.full((depth, rows), depth_ref[tile_index * across + tile], jnp.int32)
            target[3 * levels_here, :, at] = jnp.where(shore[side, :, at] == 1, value, 0).astype(jnp.float32)


def borders(tile_depth, fields, land, depth):
    levels_here, _, cols = fields[0].shape
    count = 3 * levels_here + 1
    edge = jax.ShapeDtypeStruct((count, depth, cols), jnp.float32)
    far = pl.BlockSpec(memory_space=pltpu.HBM)
    vmem = pl.BlockSpec(memory_space=pltpu.VMEM)
    return pl.pallas_call(
        border_kernel,
        out_shape=(edge, edge),
        in_specs=[pl.BlockSpec(memory_space=pltpu.SMEM)] + [far] * 4,
        out_specs=(vmem, vmem),
        scratch_shapes=[pltpu.VMEM((2, depth, cols), jnp.int32), pltpu.SemaphoreType.DMA((2, count))],
        compiler_params=pltpu.CompilerParams(vmem_limit_bytes=2 * 1024 * 1024),
        name="borders",
    )(*(pltpu.with_memory_space_constraint(array, pltpu.HBM) for array in (tile_depth, *fields, land)))


def sideways(value, lane):
    cols = value.shape[1]
    left = jnp.where(lane > 0, pltpu.roll(value, 1, 1), 0.0)
    right = jnp.where(lane < cols - 1, pltpu.roll(value, cols - 1, 1), 0.0)
    return left, right


def evolve(fields, at, active, row, rows):
    cols = fields.shape[-1]
    f32 = jnp.float32
    lane = lax.broadcasted_iota(jnp.int32, (8, cols), 1)
    places = (row + lax.broadcasted_iota(jnp.int32, (8, LANES), 0)).astype(f32)
    total_rows = lax.axis_size("tile") * rows
    coriolis = coriolis_base + coriolis_slope * (places + 0.5) / total_rows
    coriolis = jnp.concatenate([coriolis] * (cols // LANES), axis=1)

    def around(f):
        here = fields[f, at : at + 8, :]
        return (here, fields[f, at - 1 : at + 7, :], fields[f, at + 1 : at + 9, :]) + sideways(here, lane)

    def curvature(a):
        return a[2] + a[1] + a[4] + a[3] - 4.0 * a[0]

    east, north, tracer = around(0), around(1), around(2)
    grad_east = 0.5 * (tracer[2] - tracer[1])
    grad_north = 0.5 * (tracer[4] - tracer[3])
    rate = time_step * active
    return (
        east[0] + rate * (coriolis * north[0] - grad_east + viscosity * curvature(east)),
        north[0] + rate * (-coriolis * east[0] - grad_north + viscosity * curvature(north)),
        tracer[0] + rate * (-(east[0] * grad_east + north[0] * grad_north) + diffusivity * curvature(tracer)),
    )


def interior_kernel(
    depth_ref,
    high_ref,
    east_ref,
    north_ref,
    tracer_ref,
    land_ref,
    two_ref,
    one_ref,
    low_ref,
    mid_ref,
    three_ref,
    out_east,
    out_north,
    out_tracer,
    reach,
    sheet,
    one,
    two,
    three,
    mid,
    high,
    split,
    merge,
    ends,
    fields,
    shore,
    rough,
    taps,
    sems,
):
    levels_here, rows, cols = east_ref.shape
    across = cols // rows
    f32, bf16 = jnp.float32, jnp.bfloat16
    groups = cols // 2 // STRIPS
    half = cols // 2
    pitch = sheet.shape[1] // 3
    tile_index = lax.axis_index("tile")
    first_level = lax.axis_index("group") * levels_here

    def bring(level):
        return [
            pltpu.make_async_copy(ref.at[level], fields.at[f, pl.ds(PAD, rows)], sems.at[f])
            for f, ref in enumerate((east_ref, north_ref, tracer_ref))
        ]

    taps_copy = pltpu.make_async_copy(two_ref, taps, sems.at[4])
    shore_copy = pltpu.make_async_copy(land_ref, shore, sems.at[3])
    taps_copy.start()
    shore_copy.start()
    for copy in bring(0):
        copy.start()

    channels = two_ref.shape[2]
    rough[...] = jnp.zeros_like(rough)
    inputs = one_ref.shape[0]
    kernels = [[one_ref[c, r].astype(f32) * 0.5 for r in range(3)] for c in range(inputs)]
    kernels = [[jnp.concatenate([k[r][x : x + 1] for r in range(3)], axis=0) for x in range(3)] for k in kernels]
    none = jnp.zeros((3, channels), f32)
    for c in range(inputs):
        for source in range(4):
            pair = [kernels[c][source - par] if 0 <= source - par < 3 else none for par in range(2)]
            pair = jnp.concatenate(pair, axis=1)
            for p in range(2):
                start = c * 16 + source * 4 + p
                rough[start : start + 3, p * LANES : (p + 1) * LANES] = pair
    rest = jnp.concatenate([0.5 * low_ref[...]] * 4, axis=1)
    for k in range(3):
        piece = rest.astype(bf16).astype(f32)
        rough[16 * inputs + k : 16 * inputs + k + 1, :] = piece
        rest = rest - piece
    one[...] = rough[...].astype(bf16)
    none = jnp.zeros((4, channels), f32)
    outputs = three_ref.shape[0]
    kernels = [[three_ref[c, r].astype(f32) for r in range(3)] for c in range(outputs)]
    kernels = [
        [
            jnp.concatenate([k[r][x : x + 1] for k in kernels] + [none[outputs:]], axis=0)
            for x in range(3)
        ]
        for r in range(3)
    ]
    for k in range(32):
        by, bx, par, p, py = k // 16, k // 8 % 2, k // 4 % 2, k // 2 % 2, k % 2
        row = 2 * by + py - p
        pair = [
            kernels[row][2 * bx + px - par] if 0 <= row < 3 and 0 <= 2 * bx + px - par < 3 else none
            for px in range(2)
        ]
        start = 32 * by + 16 * bx + 8 * par + 4 * p
        rough[start : start + 4, py * LANES : (py + 1) * LANES] = jnp.concatenate(pair, axis=1)
    three[...] = rough[0:64, :].astype(bf16)
    mid[...] = jnp.concatenate([0.5 * mid_ref[...]] * 4, axis=1)
    comp = lax.broadcasted_iota(jnp.int32, high.shape, 0) & 3
    value = jnp.zeros(high.shape, f32)
    for c in range(high_ref.shape[0]):
        value = jnp.where(comp == c, high_ref[c], value)
    high[...] = value
    w = lax.broadcasted_iota(jnp.int32, (3 * LANES, LANES), 0)
    x = lax.broadcasted_iota(jnp.int32, (3 * LANES, LANES), 1)
    for s in range(4):
        split[:, s * LANES : (s + 1) * LANES] = jnp.where(w == 2 * x - 3 + s + LANES, 1.0, 0.0).astype(bf16)

    taps_copy.wait()
    flat = [[(taps[r, c].astype(f32) * 0.5).T.astype(bf16) for c in range(3)] for r in range(3)]
    blank = jnp.zeros((channels, channels), bf16)
    for k in range(16):
        by, bx, py, px = k // 8, k // 4 % 2, k // 2 % 2, k % 2
        for p in range(2):
            row, column = 2 * by + py - p, 2 * bx + px
            pair = [
                flat[row][column - par] if 0 <= row < 3 and 0 <= column - par < 3 else blank
                for par in range(2)
            ]
            two[k * channels : (k + 1) * channels, p * LANES : (p + 1) * LANES] = jnp.concatenate(pair, axis=1)
    at_strip = lax.broadcasted_iota(jnp.int32, (STRIPS, LANES), 0)
    at_lane = lax.broadcasted_iota(jnp.int32, (STRIPS, LANES), 1)
    for tile in range(cols // LANES):
        inside = at_lane + tile * LANES - 2 * groups * at_strip
        for par in range(2):
            for t in range(groups):
                start = par * half + t * STRIPS
                merge[start : start + STRIPS, tile * LANES : (tile + 1) * LANES] = jnp.where(
                    inside == 2 * t + par, 1.0, 0.0
                ).astype(bf16)
    for level in range(levels_here):
        sheet[level, :, 0:LANES] = jnp.zeros((3 * pitch, LANES), f32)
        sheet[level, :, LANES + cols :] = jnp.zeros((3 * pitch, sheet.shape[2] - LANES - cols), f32)
        for f in range(3):
            low_pad = f * pitch + rows + 2 * HALO
            sheet[level, low_pad : (f + 1) * pitch, :] = jnp.zeros((pitch - rows - 2 * HALO, sheet.shape[2]), f32)
            sheet[level, f * pitch : f * pitch + HALO, :] = jnp.zeros((HALO, sheet.shape[2]), f32)
            low_pad = f * pitch + rows + HALO
            sheet[level, low_pad : low_pad + HALO, :] = jnp.zeros((HALO, sheet.shape[2]), f32)
    for f in range(3):
        fields[f, PAD - 8 : PAD, :] = jnp.zeros((8, cols), f32)
        fields[f, PAD + rows : PAD + rows + 8, :] = jnp.zeros((8, cols), f32)

    shore_copy.wait()
    depths = jnp.concatenate(
        [
            jnp.full((8, rows), depth_ref[tile_index * across + tile], jnp.int32).astype(f32)
            for tile in range(across)
        ],
        axis=1,
    )
    for r in range(0, rows, 8):
        reach[r : r + 8, :] = jnp.where(shore[r : r + 8, :] == 1, depths, 0.0)

    for level in range(levels_here):
        copies = bring(level)
        for copy in copies:
            if level:
                copy.start()
        for copy in copies:
            copy.wait()
        for f in range(3):
            ends[0, f * levels_here + level] = fields[f, PAD : PAD + 8, :]
            ends[1, f * levels_here + level] = fields[f, PAD + rows - 8 : PAD + rows, :]
        number = (first_level + level).astype(f32)
        for start in range(0, rows, 8):
            active = jnp.where(number < reach[start : start + 8, :], 1.0, 0.0)
            news = evolve(fields, start + PAD, active, tile_index * rows + start, rows)
            for f, (new, out) in enumerate(zip(news, (out_east, out_north, out_tracer), strict=True)):
                out[level, start : start + 8, :] = new
                at = f * pitch + start + HALO
                sheet[level, at : at + 8, LANES : LANES + cols] = new * active


def step_kernel(
    east_ref,
    north_ref,
    tracer_ref,
    reach_ref,
    sheet,
    one,
    two,
    three,
    mid,
    high,
    split,
    merge,
    ends,
    upper_ref,
    lower_ref,
    out_east,
    out_north,
    out_tracer,
    edges,
    rim,
    reach,
    parts,
    turned,
    ready,
    hidden,
    top,
    sums,
    stress,
    natural,
):
    levels_here, rows, cols = east_ref.shape
    depth = upper_ref.shape[1]
    f32, bf16 = jnp.float32, jnp.bfloat16
    groups = cols // 2 // STRIPS
    half = cols // 2
    rows_two = (groups + 1) * STRIPS
    pitch = sheet.shape[1] // 3
    windows = -(-(half + 2) // LANES)
    turns = (rows // 2 + 2) // TURN
    strip = groups + 3
    lane = lax.broadcasted_iota(jnp.int32, (8, cols), 1)
    sub = lax.broadcasted_iota(jnp.int32, (8, LANES), 0)
    line = lax.broadcasted_iota(jnp.int32, (8, cols), 0)
    first_row = lax.axis_index("tile") * rows
    first_level = lax.axis_index("group") * levels_here

    columns = lax.broadcasted_iota(jnp.int32, turned.shape, 2)
    turned[...] = jnp.where((columns >= 48) & (columns < 51), 1.0, 0.0)
    for s in range(4):
        for m in range(windows):
            parts[s, m, 0:LEAD, :] = jnp.zeros((LEAD, LANES), f32)
            parts[s, m, LEAD + 3 * pitch :, :] = jnp.zeros((parts.shape[2] - LEAD - 3 * pitch, LANES), f32)
    reach[PAD - 8 : PAD, :] = upper_ref[3 * levels_here]
    reach[PAD + rows : PAD + rows + 8, :] = lower_ref[3 * levels_here]
    for r in range(0, rows, 8):
        reach[PAD + r : PAD + r + 8, :] = reach_ref[r : r + 8, :]

    def wet(number, at):
        return jnp.where(number < reach[at : at + 8, :], 1.0, 0.0)

    def rims(level, number):
        fixed = {}
        zero = jnp.zeros((8, cols), f32)
        rim[:, 0:LANES] = jnp.zeros((rim.shape[0], LANES), f32)
        rim[:, LANES + cols :] = jnp.zeros((rim.shape[0], rim.shape[1] - LANES - cols), f32)
        for side, (outer, inner, start) in enumerate(
            ((upper_ref, ends.at[0], -8), (ends.at[1], lower_ref, rows - 8))
        ):
            for f in range(3):
                edges[f, 0:8, :] = zero
                edges[f, 8:16, :] = outer[f * levels_here + level]
                edges[f, 16:24, :] = inner[f * levels_here + level]
                edges[f, 24:32, :] = zero
            active = [wet(number, start + PAD + r) for r in (0, 8)]
            news = [evolve(edges, 8 + r, active[r // 8], first_row + start + r, rows) for r in (0, 8)]
            for f, ref in enumerate((east_ref, north_ref, tracer_ref)):
                if side == 0:
                    kept = jnp.where(line == 0, news[1][f], ref[level, 0:8, :])
                    features = jnp.concatenate([(news[0][f] * active[0])[8 - HALO :], (kept * active[1])[:HALO]])
                else:
                    kept = jnp.where(line == 7, news[0][f], ref[level, rows - 8 : rows, :])
                    features = jnp.concatenate([(kept * active[0])[8 - HALO :], (news[1][f] * active[1])[:HALO]])
                fixed[f, side] = kept
                at = (3 * side + f) * 8
                rim[at : at + 8, LANES : LANES + cols] = features
        for f, out in enumerate((out_east, out_north, out_tracer)):
            out[level, 0:8, :] = fixed[f, 0]
            out[level, rows - 8 : rows, :] = fixed[f, 1]
        for start in range(8, rows - 8, 8):
            out_tracer[level, start : start + 8, :] = tracer_ref[level, start : start + 8, :]

    def split_columns(level):
        for m in range(windows):
            wide = min(3, (LANES + cols) // LANES - 2 * m) * LANES
            at = slice(2 * m * LANES, 2 * m * LANES + wide)
            pieces = jnp.dot(sheet[level, :, at].astype(bf16), split[0:wide, :], preferred_element_type=f32)
            for s in range(4):
                parts[s, m, LEAD : LEAD + 3 * pitch, :] = pieces[:, s * LANES : (s + 1) * LANES]
        for m in range(windows):
            at = slice(2 * m * LANES, (2 * m + 3) * LANES)
            pieces = jnp.dot(rim[:, at].astype(bf16), split[...], preferred_element_type=f32)
            for s in range(4):
                for side in range(2):
                    for f in range(3):
                        start, from_ = LEAD + f * pitch + side * rows, (3 * side + f) * 8
                        parts[s, m, start : start + 8, :] = pieces[from_ : from_ + 8, s * LANES : (s + 1) * LANES]

    def prepare(slot, base, offset):
        flipped, twin = [], slot % 2
        for m in range(windows):
            at = lambda s, first: parts[s, m, pl.ds(base + first, 8), :]
            stack = jnp.concatenate(
                [
                    jnp.where(
                        sub < 4,
                        at(s, LEAD + c * pitch + offset),
                        at(s + 1, LEAD + c * pitch + offset - 4),
                    )
                    for c in range(3)
                    for s in (0, 2)
                ],
                axis=0,
            )
            flipped.append(stack.T)
        flipped = jnp.concatenate(flipped, axis=0)
        for s in range(STRIPS):
            turned[twin, s * strip : s * strip + groups + 8, 0:48] = flipped[s * groups : (s + 1) * groups + 8]
        for t in range(groups + 2):
            ready[slot, t * STRIPS : (t + 1) * STRIPS, :] = turned[twin, pl.ds(t, STRIPS, strip), :].astype(bf16)

    def layer_one(slot, target):
        value = jnp.dot(ready[slot], one[...], preferred_element_type=f32)
        hidden[target] = gate(value).astype(bf16)

    def layer_two(slot):
        gathered = jnp.concatenate(
            [hidden[slot + by, bx * STRIPS : bx * STRIPS + rows_two, :] for by in range(2) for bx in range(2)],
            axis=1,
        )
        value = jnp.dot(gathered, two[...], preferred_element_type=f32)
        top[slot, 0:rows_two, :] = gate(value + mid[...]).astype(bf16)

    def tails():
        rows = jnp.concatenate([top[slot, half:rows_two, :] for slot in range(TURN)], axis=0)
        return lax.dot_general(three[...], rows, (((1,), (1,)), ((), ())), preferred_element_type=f32)

    def layer_three(slot, base, offset, tail):
        new = lax.dot_general(
            three[...], top[slot, 0:half, :], (((1,), (1,)), ((), ())), preferred_element_type=f32
        )
        new = jnp.concatenate([new, tail[:, slot * STRIPS : (slot + 1) * STRIPS]], axis=1)
        old = sums[...]
        wide = old[16:32, STRIPS : STRIPS + half] + new[48:64, STRIPS : STRIPS + half]
        value = old[0:16, 0:half] + new[32:48, 0:half] + wide + high[...]
        stress[pl.ds(base + offset, 8), 0:half] = value[0:8]
        stress[pl.ds(base + offset, 8), half:cols] = value[8:16]
        sums[...] = new

    def finish(level, number):
        merged = jnp.dot(stress[8 * (TURN + 1) :, :].astype(bf16), merge[...], preferred_element_type=f32)
        for tile in range(cols // LANES):
            natural[tile] = merged[:, tile * LANES : (tile + 1) * LANES]

        def field(start, shift, comp):
            at = pl.ds(4 * (start + 1 + shift) + comp, 8, 4)
            value = jnp.concatenate([natural[tile, at, :] for tile in range(cols // LANES)], axis=1)
            return value * wet(number, start + PAD + shift)

        for start in range(0, rows, 8):
            rate = eddy_gain * wet(number, start + PAD)
            east_left, east_right = sideways(field(start, 0, 1), lane)
            north_left, north_right = sideways(field(start, 0, 2), lane)
            push_east = 0.5 * (field(start, 1, 0) - field(start, -1, 0)) + 0.5 * (east_right - east_left)
            push_north = 0.5 * (field(start, 1, 1) - field(start, -1, 1)) + 0.5 * (north_right - north_left)
            inside = 0 < start < rows - 8
            for out, ref, push in ((out_east, east_ref, push_east), (out_north, north_ref, push_north)):
                base = (ref if inside else out)[level, start : start + 8, :]
                out[level, start : start + 8, :] = base + rate * push

    for level in range(levels_here):
        number = (first_level + level).astype(f32)
        rims(level, number)
        split_columns(level)
        for slot in range(TURN + 1):
            prepare(slot % TURN, 0, 2 * slot)
            layer_one(slot % TURN, slot)
        for slot in range(TURN):
            prepare(slot, 0, 2 * (TURN + 1 + slot))

        def turn(k, carry):
            at = pl.multiple_of(8 * TURN * k, 16)
            base = 2 * TURN * k
            tail = tails()
            for i in range(TURN):
                layer_three(i, at, 8 * i, tail)
                layer_two(i)
                if i:
                    layer_one(i - 1, i)
                    prepare(i - 1, base, 2 * (2 * TURN + i))
            hidden[0] = hidden[TURN]
            layer_one(TURN - 1, TURN)
            prepare(TURN - 1, base, 6 * TURN)
            return carry

        lax.fori_loop(0, turns, turn, 0)
        tail = tails()
        for i in range(TURN):
            layer_three(i, 8 * TURN * turns, 8 * i, tail)
        finish(level, number)


def ocean_step(tile_depth, fields, land, upper, lower, weights):
    conv_one, bias_one, conv_two, bias_two, conv_three, bias_three = weights
    levels_here, rows, cols = fields[0].shape
    hidden = conv_two.shape[0]
    width = 4 * hidden
    half = cols // 2
    groups = half // STRIPS
    windows = -(-(half + 2) // LANES)
    turns = (rows // 2 + 2) // TURN
    pitch = rows + 4 * HALO
    f32, bf16 = jnp.float32, jnp.bfloat16
    one = conv_one.transpose(1, 2, 3, 0)
    two = conv_two.transpose(2, 3, 0, 1)
    three = conv_three.transpose(0, 2, 3, 1)
    vmem = pl.BlockSpec(memory_space=pltpu.VMEM)
    smem = pl.BlockSpec(memory_space=pltpu.SMEM)
    far = pl.BlockSpec(memory_space=pltpu.HBM)
    shape = jax.ShapeDtypeStruct
    field = shape(fields[0].shape, f32)
    top_rows = (groups + 1) * STRIPS
    stress_rows = 8 * TURN * (turns + 1)
    inside = pl.pallas_call(
        interior_kernel,
        out_shape=(
            field,
            field,
            field,
            shape((rows, cols), f32),
            shape((levels_here, 3 * pitch, (2 * windows + 1) * LANES), f32),
            shape((LANES, width), bf16),
            shape((4 * width, width), bf16),
            shape((64, width), bf16),
            shape((1, width), f32),
            shape((16, half), f32),
            shape((3 * LANES, 4 * LANES), bf16),
            shape((cols, cols), bf16),
            shape((2, 3 * levels_here, 8, cols), f32),
        ),
        in_specs=[smem, smem] + [far] * 5 + [vmem] * 4,
        out_specs=(vmem,) * 13,
        scratch_shapes=[
            pltpu.VMEM((3, rows + 2 * PAD, cols), f32),
            pltpu.VMEM((rows, cols), jnp.int32),
            pltpu.VMEM((LANES, width), f32),
            pltpu.VMEM(two.shape, bf16),
            pltpu.SemaphoreType.DMA((5,)),
        ],
        cost_estimate=pl.CostEstimate(flops=20_000_000, bytes_accessed=12_000_000, transcendentals=0),
        compiler_params=pltpu.CompilerParams(vmem_limit_bytes=16 * 1024 * 1024),
        name="inside",
    )(
        *(
            pltpu.with_memory_space_constraint(array, pltpu.HBM)
            for array in (tile_depth, bias_three, *fields, land, two, one, bias_one[None], bias_two[None], three)
        )
    )
    return pl.pallas_call(
        step_kernel,
        out_shape=(field,) * 3,
        in_specs=[vmem] * 15,
        out_specs=(vmem,) * 3,
        scratch_shapes=[
            pltpu.VMEM((3, 32, cols), f32),
            pltpu.VMEM((48, (2 * windows + 1) * LANES), f32),
            pltpu.VMEM((rows + 2 * PAD, cols), f32),
            pltpu.VMEM((4, windows, LEAD + 3 * pitch + 8 * TURN, LANES), f32),
            pltpu.VMEM((2, STRIPS * (groups + 3) + 8, LANES), f32),
            pltpu.VMEM((TURN, (groups + 2) * STRIPS, LANES), bf16),
            pltpu.VMEM((TURN + 1, (groups + 2) * STRIPS, width), bf16),
            pltpu.VMEM((TURN, top_rows, width), bf16),
            pltpu.VMEM((64, top_rows), f32),
            pltpu.VMEM((stress_rows, cols), f32),
            pltpu.VMEM((cols // LANES, stress_rows - 8 * (TURN + 1), LANES), f32),
        ],
        compiler_params=pltpu.CompilerParams(vmem_limit_bytes=40 * 1024 * 1024),
        name="step",
    )(*inside, upper, lower)


def body(
    velocity_u,
    velocity_v,
    tracer,
    land,
    tile_depth,
    conv_one,
    bias_one,
    conv_two,
    bias_two,
    conv_three,
    bias_three,
):
    fields = (velocity_u, velocity_v, tracer)
    tile_count = lax.axis_size("tile")
    forward = [(i, i + 1) for i in range(tile_count - 1)]
    backward = [(target, source) for source, target in forward]
    first, last = borders(tile_depth, fields, land, EDGE)
    upper = lax.ppermute(last, "tile", forward)
    lower = lax.ppermute(first, "tile", backward)
    weights = (conv_one, bias_one, conv_two, bias_two, conv_three, bias_three)
    return ocean_step(tile_depth, fields, land, upper, lower, weights)


def solution(mesh):
    field = P("group", "tile", None)
    in_specs = (field, field, field, P("tile", None)) + (P(),) * 7
    return jax.shard_map(
        body, mesh=mesh, in_specs=in_specs, out_specs=(field,) * 3, check_vma=False
    )
```
